128 devices in a mesh: gx: 8 (over z, core), gy: 16 (over x, y).
Axes of the slice: x: 4, y: 4, z: 4, core: 2. Of those that a mesh axis runs over, the one named last changes fastest.
Arguments:
- partials: float32 [131072, 512], P(('gx', 'gy')), may hold values from -5 to 5
- partial_ids: int32 [128, 1024], replicated, may hold values from 0 to 127
- read_lists: int32 [128, 4096], replicated, may hold values from 0 to 127
- sources: int32 [128, 8192], P(('gx', 'gy')), may hold values from 0 to 4095
- targets: int32 [128, 8192], P(('gx', 'gy')), may hold values from 0 to 127
- kernels: float32 [8, 512, 512], replicated, may hold values from -0.03125 to 0.03125
Outputs:
- local_expansions: float32 [16384, 512], P(('gx', 'gy'))
The draws below stay inside these ranges and needn't reach their ends.
All inputs are finite; a program needn't handle non-finite values.
Results may differ from the reference program's by a relative error of at most 0.0003.
Values sent between devices are 32-bit elements; how exact they have to be, the bound alone decides.
No kernel may reach another device: no remote copies, remote signals or barrier semaphores. Data moves between devices by JAX's collectives and lax.ppermute only.
A program may use at most 192 MiB of HBM per device.

```python
import jax
import jax.numpy as jnp
from jax import lax

P_SIZE = 512
OCT_DEV = 128
LIST_DEV = 8192
DIRS = 8
SLOTS = 1024
READS = 4096
N_GX = 8
N_GY = 16
DEVICES = 128


def set_ends(array, own_key, low, top_value):
    extent = array.shape
    spot = [jax.random.randint(jax.random.fold_in(own_key, axis), (), 0, extent[axis]) for axis in range(len(extent))]
    array = array.at[tuple(spot)].set(low)
    longest = extent.index(max(extent))
    spot[longest] = (spot[longest] + 1) % extent[longest]
    return array.at[tuple(spot)].set(top_value)


def levels(rng, dims, pieces, least, largest):
    loudness, own = 1.0, jax.random.fold_in(rng, 6)
    for position, blocks in pieces:
        heights = jnp.exp(jax.random.uniform(jax.random.fold_in(own, position), (blocks,), jnp.float32, least / len(pieces), largest / len(pieces)))
        loudness = loudness * jnp.repeat(heights, dims[position] // blocks).reshape([-1 if axis == position else 1 for axis in range(len(dims))])
    return loudness


def scatter_about(own_key, extent, scale, most, split=(), kind=jnp.bfloat16):
    entries = scale * jax.random.normal(own_key, extent, jnp.float32)
    if split:
        entries = entries * levels(own_key, extent, split, -0.22, 0.18)
    return jnp.clip(entries, -most, most).astype(kind)


def setup_inputs(seed: int = 0) -> dict:
    key_of = jax.random.split(jax.random.key(seed), 7)
    partials = scatter_about(key_of[0], (DEVICES * SLOTS, P_SIZE), ((OCT_DEV / SLOTS) ** 0.5), 5.0, ((0, 128),), jnp.float32)
    partial_ids = set_ends(jax.random.randint(key_of[1], (DEVICES, SLOTS), 0, OCT_DEV), jax.random.fold_in(key_of[1], 1), 0, OCT_DEV - 1).astype(jnp.int32)
    read_lists = set_ends(jax.random.randint(key_of[2], (DEVICES, READS), 0, OCT_DEV), jax.random.fold_in(key_of[2], 1), 0, OCT_DEV - 1).astype(jnp.int32)
    sources = set_ends(jax.random.randint(key_of[3], (DEVICES, LIST_DEV), 0, READS), jax.random.fold_in(key_of[3], 1), 0, READS - 1).astype(jnp.int32)
    targets = set_ends(jax.random.randint(key_of[4], (DEVICES, LIST_DEV), 0, OCT_DEV), jax.random.fold_in(key_of[4], 1), 0, OCT_DEV - 1).astype(jnp.int32)
    kernels = scatter_about(key_of[5], (DIRS, P_SIZE, P_SIZE), (P_SIZE * LIST_DEV // OCT_DEV) ** -0.5, 0.03125, (), jnp.float32)
    return {"partials": partials, "partial_ids": partial_ids, "read_lists": read_lists, "sources": sources, "targets": targets, "kernels": kernels}


def reference(partials, partial_ids, read_lists, sources, targets, kernels):
    devices = N_GX * N_GY
    width = partials.shape[1]
    slots = partial_ids.shape[1]
    per_owner = slots // devices
    owner_base = (jnp.arange(slots, dtype=jnp.int32) // per_owner) * OCT_DEV
    global_ids = (owner_base[None, :] + partial_ids).reshape(-1).astype(jnp.int32)
    density = jax.ops.segment_sum(partials, global_ids, num_segments=OCT_DEV * devices)
    reads = read_lists.shape[1]
    per_reader = reads // devices
    read_base = (jnp.arange(reads, dtype=jnp.int32) // per_reader) * OCT_DEV
    kernels32 = kernels.astype(jnp.float32)

    def one_reader(inputs):
        own_reads, own_sources, own_targets = inputs
        slot_global = (read_base + own_reads).astype(jnp.int32)
        entry_rows = jnp.take(density, slot_global[own_sources], axis=0)
        grouped = entry_rows.reshape(DIRS, -1, width)
        images = jnp.einsum("dkp,dqp->dkq", grouped, kernels32, precision=lax.Precision.HIGHEST)
        return jax.ops.segment_sum(images.reshape(-1, width), own_targets, num_segments=OCT_DEV)

    result = lax.map(one_reader, (read_lists, sources, targets))
    return result.reshape(-1, width)
```

```python
import jax
import jax.numpy as jnp
from jax import lax
from jax.experimental import pallas as pl
from jax.experimental.pallas import tpu as pltpu
from jax.sharding import PartitionSpec as P

AXES = ("gx", "gy")
RING = 4
CORES = 2
OCT = 128
PER = 32
DIRS = 8
WIDTH = 512
HALF = WIDTH // 2
PLANE = RING * RING * CORES
COLS = PLANE * PER
BF16 = jnp.bfloat16
F32 = jnp.float32


def device_of(x, y, z, c):
    return ((z % RING) * CORES + c % CORES) * RING * RING + (x % RING) * RING + y % RING


def fetch(value, shift):
    pairs = []
    for z in range(RING):
        for c in range(CORES):
            for x in range(RING):
                for y in range(RING):
                    dx, dy, dz, dc = shift(c)
                    pairs.append((device_of(x + dx, y + dy, z + dz, c + dc), device_of(x, y, z, c)))
    return lax.ppermute(value, AXES, pairs)


def split(value):
    high = lax.reduce_precision(value, 8, 7)
    return high.astype(BF16), (value - high).astype(BF16)


def count_kernel(row_ref, col_ref, out_ref, rest_hbm, flag_ref, rest_ref):
    step = pl.program_id(0)
    inner = row_ref.shape[2]
    rows = lax.broadcasted_iota(jnp.int32, (2 * OCT, inner), 0)
    cols = lax.broadcasted_iota(jnp.int32, (COLS // 2, inner), 0)
    row_hot = jnp.where(rows == row_ref[0], 1.0, 0.0).astype(BF16)
    col_hot = jnp.where(cols == col_ref[0], 1.0, 0.0).astype(BF16)
    counts = lax.dot_general(
        row_hot, col_hot, (((1,), (1,)), ((), ())), preferred_element_type=F32
    )
    rounded = counts.astype(BF16)
    out_ref[0, :, : COLS // 2] = rounded[:OCT]
    out_ref[0, :, COLS // 2 :] = rounded[OCT:]
    large = jnp.max(counts) > 256.0
    flag_ref[step] = large.astype(jnp.int32)

    @pl.when(large)
    def _():
        rest = (counts - rounded.astype(F32)).astype(BF16)
        rest_ref[:, : COLS // 2] = rest[:OCT]
        rest_ref[:, COLS // 2 :] = rest[OCT:]
        start = pl.multiple_of((step % DIRS) * OCT, OCT)
        pltpu.sync_copy(rest_ref, rest_hbm.at[step // DIRS, pl.ds(start, OCT), :])


def count(row_codes, col_codes):
    steps, inner = RING * DIRS, row_codes.shape[-1]
    shape = (RING, DIRS * OCT, COLS)
    return pl.pallas_call(
        count_kernel,
        grid=(steps,),
        in_specs=[pl.BlockSpec((1, 1, inner), lambda i: (i, 0, 0))] * 2,
        out_specs=[
            pl.BlockSpec((1, OCT, COLS), lambda i: (i // DIRS, i % DIRS, 0)),
            pl.BlockSpec(memory_space=pl.ANY),
            pl.BlockSpec(memory_space=pltpu.SMEM),
        ],
        out_shape=[
            jax.ShapeDtypeStruct(shape, BF16),
            jax.ShapeDtypeStruct(shape, BF16),
            jax.ShapeDtypeStruct((steps,), jnp.int32),
        ],
        scratch_shapes=[pltpu.VMEM((OCT, COLS), BF16)],
        cost_estimate=pl.CostEstimate(
            flops=2 * steps * OCT * inner * COLS, bytes_accessed=8 << 20, transcendentals=0
        ),
        name="count",
    )(row_codes, col_codes)


def m2l_kernel(
    flag_ref, ids_ref, m0, m1, m2, m3, r0, r1, r2, r3, c_hbm, rest_hbm, kh_hbm, kl_hbm,
    out_ref,
    mine, recv, rows, counts, kh, kl, xh, xl, rest, sems,
):
    copies = []
    for i, ref in enumerate((m0, m1, m2, m3)):
        copies.append(pltpu.make_async_copy(ref, mine.at[i], sems.at[i]))
    for i, ref in enumerate((r0, r1, r2, r3)):
        copies.append(pltpu.make_async_copy(ref, recv.at[i], sems.at[RING + i]))
    late = [
        pltpu.make_async_copy(c_hbm, counts, sems.at[2 * RING]),
        pltpu.make_async_copy(kh_hbm, kh, sems.at[2 * RING + 1]),
        pltpu.make_async_copy(kl_hbm, kl, sems.at[2 * RING + 2]),
    ]
    for copy in copies + late:
        copy.start()
    for copy in copies:
        copy.wait()

    @pl.loop(0, PLANE)
    def _(owner):
        s, f, w = owner // (RING * CORES), (owner // CORES) % RING, owner % CORES
        own = mine[s, pl.ds(pl.multiple_of((f * CORES + w) * OCT, OCT), OCT), :]
        far = recv[f, pl.ds(pl.multiple_of((s * CORES + 1 - w) * OCT, OCT), OCT), :]
        own_h, far_h = own.astype(BF16), far.astype(BF16)
        own_l = (own - own_h.astype(F32)).astype(BF16)
        far_l = (far - far_h.astype(F32)).astype(BF16)
        table = jnp.concatenate([own_h, far_h, own_l, far_l], axis=1)
        octants = lax.broadcasted_iota(jnp.int32, (OCT, RING * PER), 0)
        hot = jnp.where(octants == ids_ref[pl.ds(owner, 1), :], 1.0, 0.0).astype(BF16)
        picked = lax.dot_general(
            hot, table, (((0,), (0,)), ((), ())), preferred_element_type=F32
        ).astype(BF16)
        start = pl.multiple_of(owner * PER, PER)
        for k in range(RING):
            rows[k, pl.ds(start, PER), :] = picked[k * PER : (k + 1) * PER]

    late[0].wait()

    @pl.loop(0, RING)
    def _(k):
        base = pl.multiple_of(k * OCT, OCT)

        @pl.loop(0, 2)
        def _(m):
            start = pl.multiple_of(m * (DIRS // 2) * OCT, OCT)
            both = jnp.dot(
                counts[k, pl.ds(start, DIRS // 2 * OCT), :], rows[k], preferred_element_type=F32
            )
            total = both[:, :WIDTH] + both[:, WIDTH:]
            high = total.astype(BF16)
            low = (total - high.astype(F32)).astype(BF16)
            for j in range(DIRS // 2):
                d = m * (DIRS // 2) + j
                xh[d, pl.ds(base, OCT), :] = high[j * OCT : (j + 1) * OCT]
                xl[d, pl.ds(base, OCT), :] = low[j * OCT : (j + 1) * OCT]

        @pl.loop(0, DIRS)
        def _(d):
            @pl.when(flag_ref[k * DIRS + d] != 0)
            def _():
                start = pl.multiple_of(d * OCT, OCT)
                pltpu.sync_copy(rest_hbm.at[k, pl.ds(start, OCT), :], rest)
                both = jnp.dot(rest[...], rows[k], preferred_element_type=F32)
                total = both[:, :WIDTH] + both[:, WIDTH:]
                total += xh[d, pl.ds(base, OCT), :].astype(F32)
                total += xl[d, pl.ds(base, OCT), :].astype(F32)
                high = total.astype(BF16)
                xh[d, pl.ds(base, OCT), :] = high
                xl[d, pl.ds(base, OCT), :] = (total - high.astype(F32)).astype(BF16)

    late[1].wait()
    late[2].wait()
    out_ref[...] = jnp.zeros_like(out_ref)

    @pl.loop(0, DIRS)
    def _(d):
        total = jnp.dot(xh[d], kh[d], preferred_element_type=F32)
        total += jnp.dot(xh[d], kl[d], preferred_element_type=F32)
        total += jnp.dot(xl[d], kh[d], preferred_element_type=F32)
        out_ref[...] += total


def m2l(flags, ids, mine, recv, counts, rest, kh, kl):
    anywhere = pl.BlockSpec(memory_space=pl.ANY)
    return pl.pallas_call(
        m2l_kernel,
        in_specs=[
            pl.BlockSpec(memory_space=pltpu.SMEM),
            pl.BlockSpec(memory_space=pltpu.VMEM),
        ]
        + [anywhere] * 12,
        out_specs=pl.BlockSpec(memory_space=pltpu.VMEM),
        out_shape=jax.ShapeDtypeStruct((RING * OCT, WIDTH), F32),
        scratch_shapes=[
            pltpu.VMEM((RING, RING * CORES * OCT, HALF), F32),
            pltpu.VMEM((RING, RING * CORES * OCT, HALF), F32),
            pltpu.VMEM((RING, COLS, 2 * WIDTH), BF16),
            pltpu.VMEM((RING, DIRS * OCT, COLS), BF16),
            pltpu.VMEM((DIRS, WIDTH, WIDTH), BF16),
            pltpu.VMEM((DIRS, WIDTH, WIDTH), BF16),
            pltpu.VMEM((DIRS, RING * OCT, WIDTH), BF16),
            pltpu.VMEM((DIRS, RING * OCT, WIDTH), BF16),
            pltpu.VMEM((OCT, COLS), BF16),
            pltpu.SemaphoreType.DMA((2 * RING + 3,)),
        ],
        compiler_params=pltpu.CompilerParams(vmem_limit_bytes=58 << 20),
        cost_estimate=pl.CostEstimate(
            flops=16_000_000_000, bytes_accessed=26 << 20, transcendentals=0
        ),
        name="m2l",
    )(flags, ids, *mine, *recv, counts, rest, kh, kl)


def body(partials, partial_ids, read_lists, sources, targets, kernels):
    gx, gy = lax.axis_index("gx"), lax.axis_index("gy")
    device = gx * (RING * RING) + gy
    z, c, x, y = gx // CORES, gx % CORES, gy // RING, gy % RING
    owners = lax.axis_size(AXES)
    per_owner = partials.shape[0] // owners

    lists = jnp.concatenate([sources, targets], axis=0)
    ring_lists = [lists] + [fetch(lists, lambda core, k=k: (0, 0, k, 0)) for k in range(1, RING)]

    received = lax.all_to_all(partials, AXES, split_axis=0, concat_axis=0, tiled=True)

    stacked = jnp.stack(ring_lists)
    slot, target = stacked[:, 0], stacked[:, 1]
    owner = slot // PER
    dx = (owner // RING - x) % RING
    dy = (owner - y) % RING
    s = jnp.where(c == 0, dy, dx)
    f = jnp.where(c == 0, dx, dy)
    w = (owner // (RING * RING) + c) % CORES
    column = ((s * RING + f) * CORES + w) * PER + slot % PER
    here = owner // PLANE == z
    row_codes = jnp.where(here, column // (COLS // 2) * OCT + target, -1)
    col_codes = column % (COLS // 2)
    per_dir = sources.shape[1] // DIRS
    counts, rest, flags = count(
        row_codes.reshape(RING * DIRS, 1, per_dir), col_codes.reshape(RING * DIRS, 1, per_dir)
    )

    number = jnp.arange(PLANE, dtype=jnp.int32)
    s, f, w = number // (RING * CORES), number // CORES % RING, number % CORES
    there_x = (x + jnp.where(c == 0, f, s)) % RING
    there_y = (y + jnp.where(c == 0, s, f)) % RING
    order = ((w + c) % CORES) * (RING * RING) + there_x * RING + there_y
    reads = [
        lax.dynamic_slice(
            read_lists, (((z + k) % RING * CORES + c) * (RING * RING) + gy, z * COLS), (1, COLS)
        )
        for k in range(RING)
    ]
    reads = jnp.concatenate(reads, axis=0).reshape(RING, PLANE, PER)
    ids = jnp.take(reads.transpose(1, 0, 2).reshape(PLANE, RING * PER), order, axis=0)

    turned = kernels.transpose(0, 2, 1)
    turned = jnp.where(c == 0, turned, jnp.roll(turned, HALF, axis=1))
    kh, kl = split(turned)

    octants = jnp.arange(OCT, dtype=jnp.int32)
    column_ids = lax.dynamic_slice_in_dim(partial_ids, device * per_owner, per_owner, 1).reshape(-1)
    selector = (octants[:, None] == column_ids[None, :]).astype(F32)
    density = jnp.dot(
        selector, received, precision=lax.Precision.HIGHEST, preferred_element_type=F32
    )

    keep = jnp.where(c == 0, density[:, :HALF], density[:, HALF:])
    give = jnp.where(c == 0, density[:, HALF:], density[:, :HALF])
    block = jnp.concatenate([keep, fetch(give, lambda core: (0, 0, 0, 1))], axis=0)
    along_f = lambda k: lambda core: (k, 0, 0, 0) if core == 0 else (0, k, 0, 0)
    along_s = lambda k: lambda core: (0, k, 0, 0) if core == 0 else (k, 0, 0, 0)
    line = jnp.concatenate([block] + [fetch(block, along_f(k)) for k in range(1, RING)], axis=0)
    mine = [line] + [fetch(line, along_s(k)) for k in range(1, RING)]
    recv = [fetch(part, lambda core: (0, 0, 0, 1)) for part in mine]

    out = m2l(flags, ids, mine, recv, counts, rest, kh, kl)
    total = out[:OCT]
    for k in range(1, RING):
        total = total + fetch(out[k * OCT : (k + 1) * OCT], lambda core, k=k: (0, 0, -k, 0))
    return total


def solution(mesh):
    return jax.shard_map(
        body,
        mesh=mesh,
        in_specs=(P(AXES, None), P(), P(), P(AXES, None), P(AXES, None), P()),
        out_specs=P(AXES, None),
        check_vma=False,
    )
```

```python
import functools

import jax
import jax.numpy as jnp
from jax import lax
from jax.experimental import pallas as pl
from jax.experimental.pallas import tpu as pltpu
from jax.sharding import PartitionSpec as P

AXES = ("gx", "gy")
RING = 4
CORES = 2
OCT = 128
PER = 32
DIRS = 8
WIDTH = 512
PLANE = RING * RING * CORES
BLOCK = CORES * RING * PER
HALF = RING // 2 * OCT
BF16 = jnp.bfloat16
F32 = jnp.float32
ANY = pl.BlockSpec(memory_space=pl.ANY)
SMEM = pl.BlockSpec(memory_space=pltpu.SMEM)
VMEM = pl.BlockSpec(memory_space=pltpu.VMEM)
PARAMS = pltpu.CompilerParams(vmem_limit_bytes=48 << 20)


def device_of(x, y, z, c):
    return ((z % RING) * CORES + c % CORES) * RING * RING + (x % RING) * RING + y % RING


def fetch(value, shift):
    pairs = []
    for z in range(RING):
        for c in range(CORES):
            for x in range(RING):
                for y in range(RING):
                    dx, dy, dz, dc = shift(c)
                    pairs.append((device_of(x + dx, y + dy, z + dz, c + dc), device_of(x, y, z, c)))
    return lax.ppermute(value, AXES, pairs)


def along_f(value, k):
    return fetch(value, lambda core: (k, 0, 0, 0) if core == 0 else (0, k, 0, 0))


def along_s(value, k):
    return fetch(value, lambda core: (0, k, 0, 0) if core == 0 else (k, 0, 0, 0))


def along_z(value, k):
    return fetch(value, lambda core: (0, 0, k, 0))


def across(value):
    return fetch(value, lambda core: (0, 0, 0, 1))


def parts(value):
    high = value.astype(BF16)
    return high, (value - high.astype(F32)).astype(BF16)


def count_kernel(row_ref, col_ref, out_ref, rest_hbm, flag_ref, rest_ref):
    reader = pl.program_id(0)
    inner = row_ref.shape[1]
    rows = lax.broadcasted_iota(jnp.int32, (RING // 2 * OCT, inner), 0)
    cols = lax.broadcasted_iota(jnp.int32, (2 * BLOCK, inner), 0)
    for d in range(DIRS):
        step = reader * DIRS + d
        row_hot = jnp.where(rows == row_ref[pl.ds(step, 1), :], 1.0, 0.0).astype(BF16)
        col_hot = jnp.where(cols == col_ref[pl.ds(step, 1), :], 1.0, 0.0).astype(BF16)
        counts = lax.dot_general(
            row_hot, col_hot, (((1,), (1,)), ((), ())), preferred_element_type=F32
        )
        rounded = counts.astype(BF16)
        for s in range(RING):
            i, j = s // 2 * OCT, s % 2 * BLOCK
            out_ref[s, 0, d * OCT : (d + 1) * OCT, :] = rounded[i : i + OCT, j : j + BLOCK]
        large = jnp.max(counts) > 256.0
        flag_ref[step] = large.astype(jnp.int32)

        @pl.when(large)
        def _():
            rest = (counts - rounded.astype(F32)).astype(BF16)
            for s in range(RING):
                i, j = s // 2 * OCT, s % 2 * BLOCK
                rest_ref[s] = rest[i : i + OCT, j : j + BLOCK]
            pltpu.sync_copy(rest_ref, rest_hbm.at[:, reader, pl.ds(d * OCT, OCT), :])


def count(row_codes, col_codes):
    steps, inner = row_codes.shape
    shape = (RING, RING, DIRS * OCT, BLOCK)
    return pl.pallas_call(
        count_kernel,
        grid=(RING,),
        in_specs=[pl.BlockSpec((steps, inner), lambda k: (0, 0))] * 2,
        out_specs=[pl.BlockSpec((RING, 1, DIRS * OCT, BLOCK), lambda k: (0, k, 0, 0)), ANY, SMEM],
        out_shape=[
            jax.ShapeDtypeStruct(shape, BF16),
            jax.ShapeDtypeStruct(shape, BF16),
            jax.ShapeDtypeStruct((steps,), jnp.int32),
        ],
        scratch_shapes=[pltpu.VMEM((RING, OCT, BLOCK), BF16)],
        compiler_params=PARAMS,
        cost_estimate=pl.CostEstimate(
            flops=2 * steps * OCT * inner * RING * BLOCK, bytes_accessed=8 << 20, transcendentals=0
        ),
        name="count",
    )(row_codes, col_codes)


def gather(ids_ref, block_refs, first, held, rows, sems):
    copies = [
        pltpu.make_async_copy(ref, held.at[i], sems.at[i]) for i, ref in enumerate(block_refs)
    ]
    for copy in copies:
        copy.start()
    octants = lax.broadcasted_iota(jnp.int32, (OCT, RING * PER), 0)
    for i, copy in enumerate(copies):
        copy.wait()
        for j in range(2):
            owner = 2 * i + j
            table = jnp.concatenate(parts(held[i, j * OCT : (j + 1) * OCT, :]), axis=1)
            ids = ids_ref[first(owner) : first(owner) + 1, :]
            hot = jnp.where(octants == ids, 1.0, 0.0).astype(BF16)
            picked = lax.dot_general(
                hot, table, (((0,), (0,)), ((), ())), preferred_element_type=F32
            ).astype(BF16)
            for k in range(RING):
                rows[k, owner * PER : (owner + 1) * PER, :] = picked[k * PER : (k + 1) * PER]


def product(counts, rows):
    both = jnp.dot(counts, rows, preferred_element_type=F32)
    return both[:, :WIDTH] + both[:, WIDTH:]


def add_rest(flag_ref, rest_hbm, blocks, k, rows, rest, add):
    @pl.loop(0, DIRS)
    def _(d):
        @pl.when(flag_ref[k * DIRS + d] != 0)
        def _():
            start = pl.multiple_of(d * OCT, OCT)
            for i, s in enumerate(blocks):
                pltpu.sync_copy(rest_hbm.at[s, k, pl.ds(start, OCT), :], rest)
                add(start, product(rest[...], rows[k, i * BLOCK : (i + 1) * BLOCK, :]))


def part_kernel(blocks, adds, *refs):
    n = len(blocks)
    flag_ref, ids_ref, refs = refs[0], refs[1], refs[2:]
    block_refs, refs = refs[: 4 * n], refs[4 * n :]
    count_refs, rest_hbm, refs = refs[:n], refs[n], refs[n + 1 :]
    if adds:
        old_ref, refs = refs[0], refs[1:]
    out_ref, held, rows, rest, sems = refs
    k = pl.program_id(0)

    @pl.when(k == 0)
    def _():
        owner_row = lambda owner: blocks[owner // 8] * 8 + owner % 8
        gather(ids_ref, block_refs, owner_row, held, rows, sems)

    for m in range(RING):
        here = slice(m * 2 * OCT, (m + 1) * 2 * OCT)
        total = old_ref[0, here, :] if adds else None
        for i in range(n):
            term = product(count_refs[i][0, 0, here, :], rows[k, i * BLOCK : (i + 1) * BLOCK, :])
            total = term if total is None else total + term
        out_ref[0, here, :] = total

    def add(start, term):
        out_ref[0, pl.ds(start, OCT), :] += term

    add_rest(flag_ref, rest_hbm, blocks, k, rows, rest, add)


def part(blocks, flags, ids, arrays, counts, rest, old=None):
    n = len(blocks)
    x_spec = pl.BlockSpec((1, DIRS * OCT, WIDTH), lambda k: (k, 0, 0))
    count_specs = [
        pl.BlockSpec((1, 1, DIRS * OCT, BLOCK), lambda k, s=s: (s, k, 0, 0)) for s in blocks
    ]
    olds = [] if old is None else [old]
    return pl.pallas_call(
        functools.partial(part_kernel, blocks, old is not None),
        grid=(RING,),
        in_specs=[SMEM, pl.BlockSpec((PLANE, RING * PER), lambda k: (0, 0))]
        + [ANY] * (4 * n)
        + count_specs
        + [ANY]
        + [x_spec] * len(olds),
        out_specs=x_spec,
        out_shape=jax.ShapeDtypeStruct((RING, DIRS * OCT, WIDTH), F32),
        scratch_shapes=[
            pltpu.VMEM((4 * n, HALF, WIDTH), F32),
            pltpu.VMEM((RING, n * BLOCK, 2 * WIDTH), BF16),
            pltpu.VMEM((OCT, BLOCK), BF16),
            pltpu.SemaphoreType.DMA((4 * n,)),
        ],
        compiler_params=PARAMS,
        cost_estimate=pl.CostEstimate(
            flops=n * 3_000_000_000, bytes_accessed=(4 * n + 8) << 20, transcendentals=0
        ),
        name="part",
    )(flags, ids, *arrays, *[counts] * n, rest, *olds)


def finish_kernel(
    block, readers, flag_ref, ids_ref, b0, b1, b2, b3, count_hbm, rest_hbm, x_hbm, k_hbm,
    out0, out1,
    held, rows, rest, counts, x, kernels, xh, xl, sems,
):
    n = len(readers)
    early = []
    for i, k in enumerate(readers):
        early.append(pltpu.make_async_copy(count_hbm.at[block, k], counts.at[i], sems.at[4 + i]))
        early.append(pltpu.make_async_copy(x_hbm.at[k], x.at[i], sems.at[4 + n + i]))
    late = [
        pltpu.make_async_copy(k_hbm.at[d], kernels.at[d], sems.at[4 + 2 * n + d])
        for d in range(DIRS)
    ]
    for copy in early + late:
        copy.start()
    owner_row = lambda owner: block * 8 + owner
    gather(ids_ref, (b0, b1, b2, b3), owner_row, held, rows, sems)
    for copy in early:
        copy.wait()
    for i, k in enumerate(readers):
        for m in range(RING):
            here = slice(m * 2 * OCT, (m + 1) * 2 * OCT)
            x[i, here, :] += product(counts[i, here, :], rows[k])

        def add(start, term, i=i):
            x[i, pl.ds(start, OCT), :] += term

        add_rest(flag_ref, rest_hbm, (block,), k, rows, rest, add)
        for d in range(DIRS):
            high, low = parts(x[i, d * OCT : (d + 1) * OCT, :])
            xh[d, i * OCT : (i + 1) * OCT, :] = high
            xl[d, i * OCT : (i + 1) * OCT, :] = low

    def dot(a, b):
        return lax.dot_general(a, b, (((1,), (1,)), ((), ())), preferred_element_type=F32)

    total = None
    for d in range(DIRS):
        late[d].wait()
        high, low = parts(kernels[d])
        term = dot(xh[d], high) + dot(xh[d], low) + dot(xl[d], high)
        total = term if total is None else total + term
    for i, out in enumerate((out0, out1)):
        out[...] = total[i * OCT : (i + 1) * OCT]


def finish(block, readers, flags, ids, arrays, counts, rest, x, kernels):
    n = len(readers)
    shape = jax.ShapeDtypeStruct((OCT, WIDTH), F32)
    return pl.pallas_call(
        functools.partial(finish_kernel, block, readers),
        in_specs=[SMEM, VMEM] + [ANY] * 8,
        out_specs=[VMEM] * 2,
        out_shape=[shape] * 2,
        scratch_shapes=[
            pltpu.VMEM((4, HALF, WIDTH), F32),
            pltpu.VMEM((RING, BLOCK, 2 * WIDTH), BF16),
            pltpu.VMEM((OCT, BLOCK), BF16),
            pltpu.VMEM((n, DIRS * OCT, BLOCK), BF16),
            pltpu.VMEM((n, DIRS * OCT, WIDTH), F32),
            pltpu.VMEM((DIRS, WIDTH, WIDTH), F32),
            pltpu.VMEM((DIRS, n * OCT, WIDTH), BF16),
            pltpu.VMEM((DIRS, n * OCT, WIDTH), BF16),
            pltpu.SemaphoreType.DMA((4 + 2 * n + DIRS,)),
        ],
        compiler_params=PARAMS,
        cost_estimate=pl.CostEstimate(
            flops=6_000_000_000, bytes_accessed=16 << 20, transcendentals=0
        ),
        name="finish",
    )(flags, ids, *arrays, counts, rest, x, kernels)


def body(partials, partial_ids, read_lists, sources, targets, kernels):
    gx, gy = lax.axis_index("gx"), lax.axis_index("gy")
    device = gx * (RING * RING) + gy
    z, c, x, y = gx // CORES, gx % CORES, gy // RING, gy % RING
    owners = lax.axis_size(AXES)
    per_owner = partials.shape[0] // owners

    lists = jnp.concatenate([sources, targets], axis=0)
    ring_lists = [lists] + [along_z(lists, k) for k in range(1, RING)]

    received = lax.all_to_all(partials, AXES, split_axis=0, concat_axis=0, tiled=True)

    stacked = jnp.stack(ring_lists)
    slot, target = stacked[:, 0], stacked[:, 1]
    owner = slot // PER
    core = (owner // (RING * RING)) % CORES
    dx = (owner // RING - x) % RING
    dy = (owner - y) % RING
    s = jnp.where(core == 0, dy, dx)
    f = jnp.where(core == 0, dx, dy)
    column = ((s % 2 * CORES + (core + c) % CORES) * RING + f) * PER + slot % PER
    here = owner // PLANE == z
    row_codes = jnp.where(here, s // 2 * OCT + target, -1)
    per_dir = sources.shape[1] // DIRS
    counts, rest, flags = count(
        row_codes.reshape(RING * DIRS, per_dir), column.reshape(RING * DIRS, per_dir)
    )

    number = jnp.arange(PLANE, dtype=jnp.int32)
    s, w, f = number // (RING * CORES), number // RING % CORES, number % RING
    core = (w + c) % CORES
    there_x = (x + jnp.where(core == 0, f, s)) % RING
    there_y = (y + jnp.where(core == 0, s, f)) % RING
    order = core * (RING * RING) + there_x * RING + there_y
    reads = [
        lax.dynamic_slice(
            read_lists,
            (((z + k) % RING * CORES + c) * (RING * RING) + gy, z * (PLANE * PER)),
            (1, PLANE * PER),
        )
        for k in range(RING)
    ]
    reads = jnp.concatenate(reads, axis=0).reshape(RING, PLANE, PER)
    ids = jnp.take(reads.transpose(1, 0, 2).reshape(PLANE, RING * PER), order, axis=0)

    received, counts, rest, flags, ids = lax.optimization_barrier(
        (received, counts, rest, flags, ids)
    )
    octants = jnp.arange(OCT, dtype=jnp.int32)
    column_ids = lax.dynamic_slice_in_dim(partial_ids, device * per_owner, per_owner, 1).reshape(-1)
    selector = (octants[:, None] == column_ids[None, :]).astype(F32)
    density = jnp.dot(
        selector, received, precision=lax.Precision.HIGHEST, preferred_element_type=F32
    )

    line = [density] + [along_f(density, k) for k in range(1, RING)]
    low, high = jnp.concatenate(line[:2], axis=0), jnp.concatenate(line[2:], axis=0)
    low1, high3 = along_s(low, 1), along_s(high, 3)
    high1, low3 = along_s(high, 1), along_s(low, 3)
    low2, high2 = along_s(low1, 1), along_s(high3, 3)
    block = [[low, high], [low1, high1], [low2, high2], [low3, high3]]
    block = [mine + [across(half) for half in mine] for mine in block]

    total = part((0,), flags, ids, block[0], counts, rest)
    total = part((1, 3), flags, ids, block[1] + block[3], counts, rest, total)
    last = (flags, ids, block[2], counts, rest, total, kernels)
    out2, out1 = finish(2, (2, 1), *last)
    out3, out0 = finish(2, (3, 0), *last)
    return out0 + along_z(out2, -2) + along_z(out1, -1) + along_z(out3, -3)


def solution(mesh):
    return jax.shard_map(
        body,
        mesh=mesh,
        in_specs=(P(AXES, None), P(), P(), P(AXES, None), P(AXES, None), P()),
        out_specs=P(AXES, None),
        check_vma=False,
    )
```

```python
import functools

import jax
import jax.numpy as jnp
from jax import lax
from jax.experimental import pallas as pl
from jax.experimental.pallas import tpu as pltpu
from jax.sharding import PartitionSpec as P

AXES = ("gx", "gy")
RING = 4
CORES = 2
OCT = 128
PER = 32
DIRS = 8
WIDTH = 512
PLANE = RING * RING * CORES
BLOCK = CORES * RING * PER
HALF = RING // 2 * OCT
BF16 = jnp.bfloat16
F32 = jnp.float32
HBM = pl.BlockSpec(memory_space=pltpu.HBM)
SMEM = pl.BlockSpec(memory_space=pltpu.SMEM)
VMEM = pl.BlockSpec(memory_space=pltpu.VMEM)
LIMIT = 24


def device_of(x, y, z, c):
    return ((z % RING) * CORES + c % CORES) * RING * RING + (x % RING) * RING + y % RING


def fetch(value, shift):
    pairs = []
    for z in range(RING):
        for c in range(CORES):
            for x in range(RING):
                for y in range(RING):
                    dx, dy, dz, dc = shift(c)
                    pairs.append((device_of(x + dx, y + dy, z + dz, c + dc), device_of(x, y, z, c)))
    return lax.ppermute(value, AXES, pairs)


def along_f(value, k):
    return fetch(value, lambda core: (k, 0, 0, 0) if core == 0 else (0, k, 0, 0))


def along_s(value, k):
    return fetch(value, lambda core: (0, k, 0, 0) if core == 0 else (k, 0, 0, 0))


def along_z(value, k):
    return fetch(value, lambda core: (0, 0, k, 0))


def across(value):
    return fetch(value, lambda core: (0, 0, 0, 1))


def parts(value):
    high = value.astype(BF16)
    return high, (value - high.astype(F32)).astype(BF16)


def count_kernel(row_ref, col_ref, out_ref, rest_hbm, flag_ref, rest_ref):
    reader = pl.program_id(0)
    inner = row_ref.shape[1]

    def counts_of(d):
        rows = lax.broadcasted_iota(jnp.int32, (RING // 2 * OCT, inner), 0)
        cols = lax.broadcasted_iota(jnp.int32, (2 * BLOCK, inner), 0)
        step = reader * DIRS + d
        row_hot = jnp.where(rows == row_ref[pl.ds(step, 1), :], 1.0, 0.0).astype(BF16)
        col_hot = jnp.where(cols == col_ref[pl.ds(step, 1), :], 1.0, 0.0).astype(BF16)
        return lax.dot_general(
            row_hot, col_hot, (((1,), (1,)), ((), ())), preferred_element_type=F32
        )

    tops = []
    for d in range(DIRS):
        counts = counts_of(d)
        rounded = counts.astype(BF16)
        for s in range(RING):
            i, j = s // 2 * OCT, s % 2 * BLOCK
            out_ref[s, 0, d * OCT : (d + 1) * OCT, :] = rounded[i : i + OCT, j : j + BLOCK]
        tops.append(jnp.max(counts, axis=0, keepdims=True))
    large = jnp.max(functools.reduce(jnp.maximum, tops)) > 256.0
    flag_ref[reader] = large.astype(jnp.int32)

    @pl.when(large)
    def _():
        @pl.loop(0, DIRS)
        def _(d):
            counts = counts_of(d)
            rest = (counts - counts.astype(BF16).astype(F32)).astype(BF16)
            for s in range(RING):
                i, j = s // 2 * OCT, s % 2 * BLOCK
                rest_ref[s] = rest[i : i + OCT, j : j + BLOCK]
            start = pl.multiple_of(d * OCT, OCT)
            pltpu.sync_copy(rest_ref, rest_hbm.at[:, reader, pl.ds(start, OCT), :])


def count(row_codes, col_codes):
    steps, inner = row_codes.shape
    shape = (RING, RING, DIRS * OCT, BLOCK)
    return pl.pallas_call(
        count_kernel,
        grid=(RING,),
        in_specs=[pl.BlockSpec((steps, inner), lambda k: (0, 0))] * 2,
        out_specs=[pl.BlockSpec((RING, 1, DIRS * OCT, BLOCK), lambda k: (0, k, 0, 0)), HBM, SMEM],
        out_shape=[
            jax.ShapeDtypeStruct(shape, BF16),
            jax.ShapeDtypeStruct(shape, BF16),
            jax.ShapeDtypeStruct((RING,), jnp.int32),
        ],
        scratch_shapes=[pltpu.VMEM((RING, OCT, BLOCK), BF16)],
        compiler_params=pltpu.CompilerParams(vmem_limit_bytes=20 << 20),
        cost_estimate=pl.CostEstimate(
            flops=100_000_000, bytes_accessed=1 << 20, transcendentals=0
        ),
        name="count",
    )(row_codes, col_codes)


def pick(ids_ref, first, refs, store):
    octants = lax.broadcasted_iota(jnp.int32, (OCT, RING * PER), 0)
    for i, ref in enumerate(refs):
        for j in range(2):
            owner = 2 * i + j
            table = jnp.concatenate(parts(ref[j * OCT : (j + 1) * OCT, :]), axis=1)
            hot = jnp.where(octants == ids_ref[first + owner : first + owner + 1, :], 1.0, 0.0)
            picked = lax.dot_general(
                hot.astype(BF16), table, (((0,), (0,)), ((), ())), preferred_element_type=F32
            ).astype(BF16)
            for k in range(RING):
                store(owner, k, picked[k * PER : (k + 1) * PER])


def gather_kernel(blocks, ids_ref, *refs):
    n = len(blocks)
    for i, s in enumerate(blocks):
        rows = refs[4 * n + i]

        def store(owner, k, values, rows=rows):
            rows[k, owner * PER : (owner + 1) * PER, :] = values

        pick(ids_ref, s * 2 * RING, refs[4 * i : 4 * i + 4], store)


def gather(blocks, ids, arrays):
    n = len(blocks)
    return pl.pallas_call(
        functools.partial(gather_kernel, blocks),
        in_specs=[VMEM] * (1 + 4 * n),
        out_specs=[VMEM] * n,
        out_shape=[jax.ShapeDtypeStruct((RING, BLOCK, 2 * WIDTH), BF16)] * n,
        compiler_params=pltpu.CompilerParams(vmem_limit_bytes=16 << 20),
        cost_estimate=pl.CostEstimate(
            flops=n * 1_500_000_000, bytes_accessed=n << 20, transcendentals=0
        ),
        name="gather",
    )(ids, *arrays)


def finish_kernel(
    readers, flag_ref, ids_ref, b0, b1, b2, b3, rows0, rows1, rows3, count_ref, k_ref, rest_hbm,
    out0, out1,
    rows2, xh, xl, rest,
):
    def store(owner, k, values):
        rows2[k, owner * PER : (owner + 1) * PER, :] = values

    pick(ids_ref, 2 * 2 * RING, (b0, b1, b2, b3), store)

    def product(counts, k):
        rows = jnp.concatenate([ref[k] for ref in (rows0, rows1, rows2, rows3)], axis=0)
        both = jnp.dot(jnp.concatenate(counts, axis=1), rows, preferred_element_type=F32)
        return both[:, :WIDTH] + both[:, WIDTH:]

    for i, k in enumerate(readers):
        there = slice(i * OCT, (i + 1) * OCT)
        for m in range(0, DIRS, 2):
            here = slice(m * OCT, (m + 2) * OCT)
            high, low = parts(product([count_ref[s, k, here, :] for s in range(RING)], k))
            for j in range(2):
                xh[m + j, there, :] = high[j * OCT : (j + 1) * OCT]
                xl[m + j, there, :] = low[j * OCT : (j + 1) * OCT]

        @pl.when(flag_ref[k] != 0)
        def _():
            @pl.loop(0, DIRS)
            def _(d):
                start = pl.multiple_of(d * OCT, OCT)
                pltpu.sync_copy(rest_hbm.at[:, k, pl.ds(start, OCT), :], rest)
                total = product([rest[s] for s in range(RING)], k)
                total += xh[d, there, :].astype(F32) + xl[d, there, :].astype(F32)
                high, low = parts(total)
                xh[d, there, :] = high
                xl[d, there, :] = low

    def dot(a, b):
        return lax.dot_general(a, b, (((1,), (1,)), ((), ())), preferred_element_type=F32)

    total = None
    for d in range(DIRS):
        high, low = parts(k_ref[d])
        term = dot(xh[d], high) + dot(xh[d], low) + dot(xl[d], high)
        total = term if total is None else total + term
    for i, out in enumerate((out0, out1)):
        out[...] = total[i * OCT : (i + 1) * OCT]


def finish(readers, flags, ids, arrays, rows, counts, kernels, rest):
    n = len(readers)
    return pl.pallas_call(
        functools.partial(finish_kernel, readers),
        in_specs=[SMEM] + [VMEM] * 10 + [HBM],
        out_specs=[VMEM] * 2,
        out_shape=[jax.ShapeDtypeStruct((OCT, WIDTH), F32)] * 2,
        scratch_shapes=[
            pltpu.VMEM((RING, BLOCK, 2 * WIDTH), BF16),
            pltpu.VMEM((DIRS, n * OCT, WIDTH), BF16),
            pltpu.VMEM((DIRS, n * OCT, WIDTH), BF16),
            pltpu.VMEM((RING, OCT, BLOCK), BF16),
        ],
        compiler_params=pltpu.CompilerParams(vmem_limit_bytes=LIMIT << 20),
        cost_estimate=pl.CostEstimate(
            flops=9_000_000_000, bytes_accessed=2 << 20, transcendentals=0
        ),
        name="finish",
    )(flags, ids, *arrays, *rows, counts, kernels, rest)


def body(partials, partial_ids, read_lists, sources, targets, kernels):
    gx, gy = lax.axis_index("gx"), lax.axis_index("gy")
    device = gx * (RING * RING) + gy
    z, c, x, y = gx // CORES, gx % CORES, gy // RING, gy % RING
    owners = lax.axis_size(AXES)
    per_owner = partials.shape[0] // owners

    received = lax.all_to_all(partials, AXES, split_axis=0, concat_axis=0, tiled=True)

    number = jnp.arange(PLANE, dtype=jnp.int32)
    s, w, f = number // (RING * CORES), number // RING % CORES, number % RING
    core = (w + c) % CORES
    there_x = (x + jnp.where(core == 0, f, s)) % RING
    there_y = (y + jnp.where(core == 0, s, f)) % RING
    order = core * (RING * RING) + there_x * RING + there_y
    reads = [
        lax.dynamic_slice(
            read_lists,
            (((z + k) % RING * CORES + c) * (RING * RING) + gy, z * (PLANE * PER)),
            (1, PLANE * PER),
        )
        for k in range(RING)
    ]
    reads = jnp.concatenate(reads, axis=0).reshape(RING, PLANE, PER)
    ids = jnp.take(reads.transpose(1, 0, 2).reshape(PLANE, RING * PER), order, axis=0)

    lists = jnp.concatenate([sources, targets], axis=0)
    ring_lists = [lists] + [along_z(lists, k) for k in range(1, RING)]

    stacked = jnp.stack(ring_lists)
    slot, target = stacked[:, 0], stacked[:, 1]
    owner = slot // PER
    core = (owner // (RING * RING)) % CORES
    dx = (owner // RING - x) % RING
    dy = (owner - y) % RING
    s = jnp.where(core == 0, dy, dx)
    f = jnp.where(core == 0, dx, dy)
    column = ((s % 2 * CORES + (core + c) % CORES) * RING + f) * PER + slot % PER
    here = owner // PLANE == z
    row_codes = jnp.where(here, s // 2 * OCT + target, -1)
    per_dir = sources.shape[1] // DIRS
    counts, rest, flags = count(
        row_codes.reshape(RING * DIRS, per_dir), column.reshape(RING * DIRS, per_dir)
    )

    received, counts, rest, flags, ids = lax.optimization_barrier(
        (received, counts, rest, flags, ids)
    )
    octants = jnp.arange(OCT, dtype=jnp.int32)
    column_ids = lax.dynamic_slice_in_dim(partial_ids, device * per_owner, per_owner, 1).reshape(-1)
    selector = (octants[:, None] == column_ids[None, :]).astype(F32)
    density = jnp.dot(
        selector, received, precision=lax.Precision.HIGHEST, preferred_element_type=F32
    )

    line = lax.optimization_barrier([density] + [along_f(density, k) for k in range(1, RING)])
    low, high = jnp.concatenate(line[:2], axis=0), jnp.concatenate(line[2:], axis=0)
    low1, high3, high1, low3 = along_s(low, 1), along_s(high, 3), along_s(high, 1), along_s(low, 3)
    rows = {}
    (rows[0],) = gather((0,), ids, [low, high, across(low), across(high)])
    low1, high3, rows[0] = lax.optimization_barrier((low1, high3, rows[0]))
    low2, high2 = along_s(low1, 1), along_s(high3, 3)
    near = [low1, high1, across(low1), across(high1), low3, high3, across(low3), across(high3)]
    rows[1], rows[3] = gather((1, 3), ids, near)
    low2, high2, rows[1], rows[3] = lax.optimization_barrier((low2, high2, rows[1], rows[3]))
    far = [low2, high2, across(low2), across(high2)]
    last = (flags, ids, far, (rows[0], rows[1], rows[3]), counts, kernels, rest)
    out2, out1 = finish((2, 1), *last)
    out3, out0 = finish((3, 0), *last)
    return out0 + along_z(out2, -2) + along_z(out1, -1) + along_z(out3, -3)


def solution(mesh):
    return jax.shard_map(
        body,
        mesh=mesh,
        in_specs=(P(AXES, None), P(), P(), P(AXES, None), P(AXES, None), P()),
        out_specs=P(AXES, None),
        check_vma=False,
    )
```

```python
import functools

import jax
import jax.numpy as jnp
from jax import lax
from jax.experimental import pallas as pl
from jax.experimental.pallas import tpu as pltpu
from jax.sharding import PartitionSpec as P

AXES = ("gx", "gy")
RING = 4
CORES = 2
OCT = 128
PER = 32
DIRS = 8
WIDTH = 512
PLANE = RING * RING * CORES
BLOCK = CORES * RING * PER
BF16 = jnp.bfloat16
F32 = jnp.float32
HBM = pl.BlockSpec(memory_space=pltpu.HBM)
SMEM = pl.BlockSpec(memory_space=pltpu.SMEM)
VMEM = pl.BlockSpec(memory_space=pltpu.VMEM)
LIMIT = 16


def device_of(x, y, z, c):
    return ((z % RING) * CORES + c % CORES) * RING * RING + (x % RING) * RING + y % RING


def fetch(value, shift):
    pairs = []
    for z in range(RING):
        for c in range(CORES):
            for x in range(RING):
                for y in range(RING):
                    dx, dy, dz, dc = shift(c)
                    pairs.append((device_of(x + dx, y + dy, z + dz, c + dc), device_of(x, y, z, c)))
    return lax.ppermute(value, AXES, pairs)


def along_f(value, k):
    return fetch(value, lambda core: (k, 0, 0, 0) if core == 0 else (0, k, 0, 0))


def along_s(value, k):
    return fetch(value, lambda core: (0, k, 0, 0) if core == 0 else (k, 0, 0, 0))


def along_z(value, k):
    return fetch(value, lambda core: (0, 0, k, 0))


def across(value):
    return fetch(value, lambda core: (0, 0, 0, 1))


def parts(value):
    high = value.astype(BF16)
    return high, (value - high.astype(F32)).astype(BF16)


def count_kernel(row_ref, col_ref, out_ref, rest_hbm, flag_ref, rest_ref):
    reader = pl.program_id(0)
    inner = row_ref.shape[1]

    def counts_of(d):
        rows = lax.broadcasted_iota(jnp.int32, (RING // 2 * OCT, inner), 0)
        cols = lax.broadcasted_iota(jnp.int32, (2 * BLOCK, inner), 0)
        step = reader * DIRS + d
        row_hot = jnp.where(rows == row_ref[pl.ds(step, 1), :], 1.0, 0.0).astype(BF16)
        col_hot = jnp.where(cols == col_ref[pl.ds(step, 1), :], 1.0, 0.0).astype(BF16)
        return lax.dot_general(
            row_hot, col_hot, (((1,), (1,)), ((), ())), preferred_element_type=F32
        )

    tops = []
    for d in range(DIRS):
        counts = counts_of(d)
        rounded = counts.astype(BF16)
        for s in range(RING):
            i, j = s // 2 * OCT, s % 2 * BLOCK
            out_ref[s, 0, d * OCT : (d + 1) * OCT, :] = rounded[i : i + OCT, j : j + BLOCK]
        tops.append(jnp.max(counts, axis=0, keepdims=True))
    large = jnp.max(functools.reduce(jnp.maximum, tops)) > 256.0
    flag_ref[reader] = large.astype(jnp.int32)

    @pl.when(large)
    def _():
        @pl.loop(0, DIRS)
        def _(d):
            counts = counts_of(d)
            rest = (counts - counts.astype(BF16).astype(F32)).astype(BF16)
            for s in range(RING):
                i, j = s // 2 * OCT, s % 2 * BLOCK
                rest_ref[s] = rest[i : i + OCT, j : j + BLOCK]
            start = pl.multiple_of(d * OCT, OCT)
            pltpu.sync_copy(rest_ref, rest_hbm.at[:, reader, pl.ds(start, OCT), :])


def count(row_codes, col_codes):
    steps, inner = row_codes.shape
    shape = (RING, RING, DIRS * OCT, BLOCK)
    return pl.pallas_call(
        count_kernel,
        grid=(RING,),
        in_specs=[pl.BlockSpec((steps, inner), lambda k: (0, 0))] * 2,
        out_specs=[pl.BlockSpec((RING, 1, DIRS * OCT, BLOCK), lambda k: (0, k, 0, 0)), HBM, SMEM],
        out_shape=[
            jax.ShapeDtypeStruct(shape, BF16),
            jax.ShapeDtypeStruct(shape, BF16),
            jax.ShapeDtypeStruct((RING,), jnp.int32),
        ],
        scratch_shapes=[pltpu.VMEM((RING, OCT, BLOCK), BF16)],
        compiler_params=pltpu.CompilerParams(vmem_limit_bytes=60 << 20),
        cost_estimate=pl.CostEstimate(
            flops=100_000_000, bytes_accessed=1 << 20, transcendentals=0
        ),
        name="count",
    )(row_codes, col_codes)


def pick(ids_ref, first, refs, store):
    octants = lax.broadcasted_iota(jnp.int32, (OCT, RING * PER), 0)
    for i, ref in enumerate(refs):
        for j in range(RING):
            owner = RING * i + j
            table = jnp.concatenate(parts(ref[j * OCT : (j + 1) * OCT, :]), axis=1)
            hot = jnp.where(octants == ids_ref[first + owner : first + owner + 1, :], 1.0, 0.0)
            picked = lax.dot_general(
                hot.astype(BF16), table, (((0,), (0,)), ((), ())), preferred_element_type=F32
            ).astype(BF16)
            for k in range(RING):
                store(owner, k, picked[k * PER : (k + 1) * PER])


def gather_kernel(blocks, ids_ref, *refs):
    n = len(blocks)
    for i, s in enumerate(blocks):
        rows = refs[2 * n + i]

        def store(owner, k, values, rows=rows):
            rows[k, owner * PER : (owner + 1) * PER, :] = values

        pick(ids_ref, s * 2 * RING, refs[2 * i : 2 * i + 2], store)


def gather(blocks, ids, arrays):
    n = len(blocks)
    return pl.pallas_call(
        functools.partial(gather_kernel, blocks),
        in_specs=[VMEM] * (1 + 2 * n),
        out_specs=[VMEM] * n,
        out_shape=[jax.ShapeDtypeStruct((RING, BLOCK, 2 * WIDTH), BF16)] * n,
        compiler_params=pltpu.CompilerParams(vmem_limit_bytes=16 << 20),
        cost_estimate=pl.CostEstimate(
            flops=n * 1_500_000_000, bytes_accessed=n << 20, transcendentals=0
        ),
        name="gather",
    )(ids, *arrays)


def product(counts, rows):
    both = jnp.dot(
        jnp.concatenate(counts, axis=1),
        jnp.concatenate(rows, axis=0),
        preferred_element_type=F32,
    )
    return both[:, :WIDTH] + both[:, WIDTH:]


def collect_kernel(blocks, count_ref, *refs):
    rows, out_ref = refs[:-1], refs[-1]

    @pl.loop(0, RING)
    def _(k):
        for m in range(0, DIRS, 2):
            here = slice(m * OCT, (m + 2) * OCT)
            out_ref[k, here, :] = product(
                [count_ref[s, k, here, :] for s in blocks], [ref[k] for ref in rows]
            )


def collect(blocks, counts, rows):
    n = len(blocks)
    return pl.pallas_call(
        functools.partial(collect_kernel, blocks),
        in_specs=[VMEM] * (1 + n),
        out_specs=VMEM,
        out_shape=jax.ShapeDtypeStruct((RING, DIRS * OCT, WIDTH), F32),
        compiler_params=pltpu.CompilerParams(vmem_limit_bytes=8 << 20),
        cost_estimate=pl.CostEstimate(
            flops=n * 2_200_000_000, bytes_accessed=n << 20, transcendentals=0
        ),
        name="collect",
    )(counts, *rows)


def finish_kernel(
    readers, flag_ref, ids_ref, b0, b1, x_ref, rows0, rows1, rows3, count_ref, k_ref, rest_hbm,
    out0, out1,
    rows2, xh, xl, rest,
):
    def store(owner, k, values):
        rows2[k, owner * PER : (owner + 1) * PER, :] = values

    pick(ids_ref, 2 * 2 * RING, (b0, b1), store)
    for i, k in enumerate(readers):
        there = slice(i * OCT, (i + 1) * OCT)
        for m in range(0, DIRS, 2):
            here = slice(m * OCT, (m + 2) * OCT)
            total = x_ref[k, here, :] + product([count_ref[2, k, here, :]], [rows2[k]])
            high, low = parts(total)
            for j in range(2):
                xh[m + j, there, :] = high[j * OCT : (j + 1) * OCT]
                xl[m + j, there, :] = low[j * OCT : (j + 1) * OCT]

        @pl.when(flag_ref[k] != 0)
        def _():
            @pl.loop(0, DIRS)
            def _(d):
                start = pl.multiple_of(d * OCT, OCT)
                pltpu.sync_copy(rest_hbm.at[:, k, pl.ds(start, OCT), :], rest)
                rows = [ref[k] for ref in (rows0, rows1, rows2, rows3)]
                total = product([rest[s] for s in range(RING)], rows)
                total += xh[d, there, :].astype(F32) + xl[d, there, :].astype(F32)
                high, low = parts(total)
                xh[d, there, :] = high
                xl[d, there, :] = low

    def dot(a, b):
        return lax.dot_general(a, b, (((1,), (1,)), ((), ())), preferred_element_type=F32)

    total = None
    for d in range(DIRS):
        high, low = parts(k_ref[d])
        term = dot(xh[d], high) + dot(xh[d], low) + dot(xl[d], high)
        total = term if total is None else total + term
    for i, out in enumerate((out0, out1)):
        out[...] = total[i * OCT : (i + 1) * OCT]


def finish(readers, flags, ids, arrays, x, rows, counts, kernels, rest):
    n = len(readers)
    return pl.pallas_call(
        functools.partial(finish_kernel, readers),
        in_specs=[SMEM] + [VMEM] * 9 + [HBM],
        out_specs=[VMEM] * 2,
        out_shape=[jax.ShapeDtypeStruct((OCT, WIDTH), F32)] * 2,
        scratch_shapes=[
            pltpu.VMEM((RING, BLOCK, 2 * WIDTH), BF16),
            pltpu.VMEM((DIRS, n * OCT, WIDTH), BF16),
            pltpu.VMEM((DIRS, n * OCT, WIDTH), BF16),
            pltpu.VMEM((RING, OCT, BLOCK), BF16),
        ],
        compiler_params=pltpu.CompilerParams(vmem_limit_bytes=LIMIT << 20),
        cost_estimate=pl.CostEstimate(
            flops=6_000_000_000, bytes_accessed=2 << 20, transcendentals=0
        ),
        name="finish",
    )(flags, ids, *arrays, x, *rows, counts, kernels, rest)


def body(partials, partial_ids, read_lists, sources, targets, kernels):
    gx, gy = lax.axis_index("gx"), lax.axis_index("gy")
    device = gx * (RING * RING) + gy
    z, c, x, y = gx // CORES, gx % CORES, gy // RING, gy % RING
    owners = lax.axis_size(AXES)
    per_owner = partials.shape[0] // owners

    received = lax.all_to_all(partials, AXES, split_axis=0, concat_axis=0, tiled=True)

    number = jnp.arange(PLANE, dtype=jnp.int32)
    s, w, f = number // (RING * CORES), number // RING % CORES, number % RING
    core = (w + c) % CORES
    there_x = (x + jnp.where(core == 0, f, s)) % RING
    there_y = (y + jnp.where(core == 0, s, f)) % RING
    order = core * (RING * RING) + there_x * RING + there_y
    reads = [
        lax.dynamic_slice(
            read_lists,
            (((z + k) % RING * CORES + c) * (RING * RING) + gy, z * (PLANE * PER)),
            (1, PLANE * PER),
        )
        for k in range(RING)
    ]
    reads = jnp.concatenate(reads, axis=0).reshape(RING, PLANE, PER)
    ids = jnp.take(reads.transpose(1, 0, 2).reshape(PLANE, RING * PER), order, axis=0)

    lists = jnp.concatenate([sources, targets], axis=0)
    ring_lists = [lists] + [along_z(lists, k) for k in range(1, RING)]

    stacked = jnp.stack(ring_lists)
    slot, target = stacked[:, 0], stacked[:, 1]
    owner = slot // PER
    core = (owner // (RING * RING)) % CORES
    dx = (owner // RING - x) % RING
    dy = (owner - y) % RING
    s = jnp.where(core == 0, dy, dx)
    f = jnp.where(core == 0, dx, dy)
    column = ((s % 2 * CORES + (core + c) % CORES) * RING + f) * PER + slot % PER
    here = owner // PLANE == z
    row_codes = jnp.where(here, s // 2 * OCT + target, -1)
    per_dir = sources.shape[1] // DIRS
    counts, rest, flags = count(
        row_codes.reshape(RING * DIRS, per_dir), column.reshape(RING * DIRS, per_dir)
    )

    octants = jnp.arange(OCT, dtype=jnp.int32)
    column_ids = lax.dynamic_slice_in_dim(partial_ids, device * per_owner, per_owner, 1).reshape(-1)
    selector = (octants[:, None] == column_ids[None, :]).astype(F32)
    density = jnp.dot(
        selector, received, precision=lax.Precision.HIGHEST, preferred_element_type=F32
    )

    line = [density] + [along_f(density, k) for k in range(1, RING)]
    line, counts, rest, flags, ids = lax.optimization_barrier((line, counts, rest, flags, ids))
    line = jnp.concatenate(line, axis=0)
    block = {1: along_s(line, 1), 3: along_s(line, 3)}
    rows = {}
    (rows[0],) = gather((0,), ids, [line, across(line)])
    line, rows[0] = lax.optimization_barrier((line, rows[0]))
    block[2] = along_s(line, 2)
    near = [block[1], across(block[1]), block[3], across(block[3])]
    rows[1], rows[3] = gather((1, 3), ids, near)
    rows = (rows[0], rows[1], rows[3])
    x = collect((0, 1, 3), counts, rows)
    block[2], x = lax.optimization_barrier((block[2], x))
    far = [block[2], across(block[2])]
    last = (flags, ids, far, x, rows, counts, kernels, rest)
    out2, out1 = finish((2, 1), *last)
    out3, out0 = finish((3, 0), *last)
    return out0 + along_z(out2, -2) + along_z(out1, -1) + along_z(out3, -3)


def solution(mesh):
    return jax.shard_map(
        body,
        mesh=mesh,
        in_specs=(P(AXES, None), P(), P(), P(AXES, None), P(AXES, None), P()),
        out_specs=P(AXES, None),
        check_vma=False,
    )
```

```python
import functools

import jax
import jax.numpy as jnp
from jax import lax
from jax.experimental import pallas as pl
from jax.experimental.pallas import tpu as pltpu
from jax.sharding import PartitionSpec as P

AXES = ("gx", "gy")
RING = 4
CORES = 2
OCT = 128
PER = 32
DIRS = 8
WIDTH = 512
PLANE = RING * RING * CORES
BLOCK = CORES * RING * PER
BF16 = jnp.bfloat16
F32 = jnp.float32
HBM = pl.BlockSpec(memory_space=pltpu.HBM)
SMEM = pl.BlockSpec(memory_space=pltpu.SMEM)
VMEM = pl.BlockSpec(memory_space=pltpu.VMEM)
LIMIT = 16


def device_of(x, y, z, c):
    return ((z % RING) * CORES + c % CORES) * RING * RING + (x % RING) * RING + y % RING


def fetch(value, shift):
    pairs = []
    for z in range(RING):
        for c in range(CORES):
            for x in range(RING):
                for y in range(RING):
                    dx, dy, dz, dc = shift(c)
                    pairs.append((device_of(x + dx, y + dy, z + dz, c + dc), device_of(x, y, z, c)))
    return lax.ppermute(value, AXES, pairs)


def along_f(value, k):
    return fetch(value, lambda core: (k, 0, 0, 0) if core == 0 else (0, k, 0, 0))


def along_s(value, k):
    return fetch(value, lambda core: (0, k, 0, 0) if core == 0 else (k, 0, 0, 0))


def along_z(value, k):
    return fetch(value, lambda core: (0, 0, k, 0))


def across(value):
    return fetch(value, lambda core: (0, 0, 0, 1))


def parts(value):
    high = value.astype(BF16)
    return high, (value - high.astype(F32)).astype(BF16)


def count_kernel(row_ref, col_ref, out_ref, rest_hbm, flag_ref, rest_ref):
    reader = pl.program_id(0)
    inner = row_ref.shape[1]

    def counts_of(d):
        rows = lax.broadcasted_iota(jnp.int32, (RING // 2 * OCT, inner), 0)
        cols = lax.broadcasted_iota(jnp.int32, (2 * BLOCK, inner), 0)
        step = reader * DIRS + d
        row_hot = jnp.where(rows == row_ref[pl.ds(step, 1), :], 1.0, 0.0).astype(BF16)
        col_hot = jnp.where(cols == col_ref[pl.ds(step, 1), :], 1.0, 0.0).astype(BF16)
        return lax.dot_general(
            row_hot, col_hot, (((1,), (1,)), ((), ())), preferred_element_type=F32
        )

    tops = []
    for d in range(DIRS):
        counts = counts_of(d)
        rounded = counts.astype(BF16)
        for s in range(RING):
            i, j = s // 2 * OCT, s % 2 * BLOCK
            out_ref[s, 0, d * OCT : (d + 1) * OCT, :] = rounded[i : i + OCT, j : j + BLOCK]
        tops.append(jnp.max(counts, axis=0, keepdims=True))
    large = jnp.max(functools.reduce(jnp.maximum, tops)) > 256.0
    flag_ref[reader] = large.astype(jnp.int32)

    @pl.when(large)
    def _():
        @pl.loop(0, DIRS)
        def _(d):
            counts = counts_of(d)
            rest = (counts - counts.astype(BF16).astype(F32)).astype(BF16)
            for s in range(RING):
                i, j = s // 2 * OCT, s % 2 * BLOCK
                rest_ref[s] = rest[i : i + OCT, j : j + BLOCK]
            start = pl.multiple_of(d * OCT, OCT)
            pltpu.sync_copy(rest_ref, rest_hbm.at[:, reader, pl.ds(start, OCT), :])


def count(row_codes, col_codes):
    steps, inner = row_codes.shape
    shape = (RING, RING, DIRS * OCT, BLOCK)
    return pl.pallas_call(
        count_kernel,
        grid=(RING,),
        in_specs=[pl.BlockSpec((steps, inner), lambda k: (0, 0))] * 2,
        out_specs=[pl.BlockSpec((RING, 1, DIRS * OCT, BLOCK), lambda k: (0, k, 0, 0)), HBM, SMEM],
        out_shape=[
            jax.ShapeDtypeStruct(shape, BF16),
            jax.ShapeDtypeStruct(shape, BF16),
            jax.ShapeDtypeStruct((RING,), jnp.int32),
        ],
        scratch_shapes=[pltpu.VMEM((RING, OCT, BLOCK), BF16)],
        compiler_params=pltpu.CompilerParams(vmem_limit_bytes=60 << 20),
        cost_estimate=pl.CostEstimate(
            flops=100_000_000, bytes_accessed=1 << 20, transcendentals=0
        ),
        name="count",
    )(row_codes, col_codes)


def pick(ids_ref, first, refs, store):
    octants = lax.broadcasted_iota(jnp.int32, (OCT, RING * PER), 0)
    many = CORES * RING // len(refs)
    for i, ref in enumerate(refs):
        for j in range(many):
            owner = many * i + j
            table = jnp.concatenate(parts(ref[j * OCT : (j + 1) * OCT, :]), axis=1)
            hot = jnp.where(octants == ids_ref[first + owner : first + owner + 1, :], 1.0, 0.0)
            picked = lax.dot_general(
                hot.astype(BF16), table, (((0,), (0,)), ((), ())), preferred_element_type=F32
            ).astype(BF16)
            for k in range(RING):
                store(owner, k, picked[k * PER : (k + 1) * PER])


def gather_kernel(blocks, ids_ref, *refs):
    n = len(blocks)
    for i, s in enumerate(blocks):
        rows = refs[2 * n + i]

        def store(owner, k, values, rows=rows):
            rows[k, owner * PER : (owner + 1) * PER, :] = values

        pick(ids_ref, s * 2 * RING, refs[2 * i : 2 * i + 2], store)


def gather(blocks, ids, arrays):
    n = len(blocks)
    return pl.pallas_call(
        functools.partial(gather_kernel, blocks),
        in_specs=[VMEM] * (1 + 2 * n),
        out_specs=[VMEM] * n,
        out_shape=[jax.ShapeDtypeStruct((RING, BLOCK, 2 * WIDTH), BF16)] * n,
        compiler_params=pltpu.CompilerParams(vmem_limit_bytes=16 << 20),
        cost_estimate=pl.CostEstimate(
            flops=n * 1_500_000_000, bytes_accessed=n << 20, transcendentals=0
        ),
        name="gather",
    )(ids, *arrays)


def product(counts, rows):
    both = jnp.dot(
        jnp.concatenate(counts, axis=1),
        jnp.concatenate(rows, axis=0),
        preferred_element_type=F32,
    )
    return both[:, :WIDTH] + both[:, WIDTH:]


def collect_kernel(blocks, count_ref, *refs):
    rows, out_ref = refs[:-1], refs[-1]

    @pl.loop(0, RING)
    def _(k):
        for m in range(0, DIRS, 2):
            here = slice(m * OCT, (m + 2) * OCT)
            out_ref[k, here, :] = product(
                [count_ref[s, k, here, :] for s in blocks], [ref[k] for ref in rows]
            )


def collect(blocks, counts, rows):
    n = len(blocks)
    return pl.pallas_call(
        functools.partial(collect_kernel, blocks),
        in_specs=[VMEM] * (1 + n),
        out_specs=VMEM,
        out_shape=jax.ShapeDtypeStruct((RING, DIRS * OCT, WIDTH), F32),
        compiler_params=pltpu.CompilerParams(vmem_limit_bytes=8 << 20),
        cost_estimate=pl.CostEstimate(
            flops=n * 2_200_000_000, bytes_accessed=n << 20, transcendentals=0
        ),
        name="collect",
    )(counts, *rows)


def finish_kernel(
    readers, flag_ref, ids_ref, b0, b1, b2, b3, x_ref, rows0, rows1, rows3, count_ref, k_ref, rest_hbm,
    out0, out1,
    rows2, xh, xl, rest,
):
    def store(owner, k, values):
        rows2[k, owner * PER : (owner + 1) * PER, :] = values

    pick(ids_ref, 2 * 2 * RING, (b0, b1, b2, b3), store)
    for i, k in enumerate(readers):
        there = slice(i * OCT, (i + 1) * OCT)
        for m in range(0, DIRS, 2):
            here = slice(m * OCT, (m + 2) * OCT)
            total = x_ref[k, here, :] + product([count_ref[2, k, here, :]], [rows2[k]])
            high, low = parts(total)
            for j in range(2):
                xh[m + j, there, :] = high[j * OCT : (j + 1) * OCT]
                xl[m + j, there, :] = low[j * OCT : (j + 1) * OCT]

        @pl.when(flag_ref[k] != 0)
        def _():
            @pl.loop(0, DIRS)
            def _(d):
                start = pl.multiple_of(d * OCT, OCT)
                pltpu.sync_copy(rest_hbm.at[:, k, pl.ds(start, OCT), :], rest)
                rows = [ref[k] for ref in (rows0, rows1, rows2, rows3)]
                total = product([rest[s] for s in range(RING)], rows)
                total += xh[d, there, :].astype(F32) + xl[d, there, :].astype(F32)
                high, low = parts(total)
                xh[d, there, :] = high
                xl[d, there, :] = low

    def dot(a, b):
        return lax.dot_general(a, b, (((1,), (1,)), ((), ())), preferred_element_type=F32)

    total = None
    for d in range(DIRS):
        high, low = parts(k_ref[d])
        term = dot(xh[d], high) + dot(xh[d], low) + dot(xl[d], high)
        total = term if total is None else total + term
    for i, out in enumerate((out0, out1)):
        out[...] = total[i * OCT : (i + 1) * OCT]


def finish(readers, flags, ids, arrays, x, rows, counts, kernels, rest):
    n = len(readers)
    return pl.pallas_call(
        functools.partial(finish_kernel, readers),
        in_specs=[SMEM] + [VMEM] * 11 + [HBM],
        out_specs=[VMEM] * 2,
        out_shape=[jax.ShapeDtypeStruct((OCT, WIDTH), F32)] * 2,
        scratch_shapes=[
            pltpu.VMEM((RING, BLOCK, 2 * WIDTH), BF16),
            pltpu.VMEM((DIRS, n * OCT, WIDTH), BF16),
            pltpu.VMEM((DIRS, n * OCT, WIDTH), BF16),
            pltpu.VMEM((RING, OCT, BLOCK), BF16),
        ],
        compiler_params=pltpu.CompilerParams(vmem_limit_bytes=LIMIT << 20),
        cost_estimate=pl.CostEstimate(
            flops=6_000_000_000, bytes_accessed=2 << 20, transcendentals=0
        ),
        name="finish",
    )(flags, ids, *arrays, x, *rows, counts, kernels, rest)


def body(partials, partial_ids, read_lists, sources, targets, kernels):
    gx, gy = lax.axis_index("gx"), lax.axis_index("gy")
    device = gx * (RING * RING) + gy
    z, c, x, y = gx // CORES, gx % CORES, gy // RING, gy % RING
    owners = lax.axis_size(AXES)
    per_owner = partials.shape[0] // owners

    received = lax.all_to_all(partials, AXES, split_axis=0, concat_axis=0, tiled=True)

    number = jnp.arange(PLANE, dtype=jnp.int32)
    s, w, f = number // (RING * CORES), number // RING % CORES, number % RING
    core = (w + c) % CORES
    there_x = (x + jnp.where(core == 0, f, s)) % RING
    there_y = (y + jnp.where(core == 0, s, f)) % RING
    order = core * (RING * RING) + there_x * RING + there_y
    reads = [
        lax.dynamic_slice(
            read_lists,
            (((z + k) % RING * CORES + c) * (RING * RING) + gy, z * (PLANE * PER)),
            (1, PLANE * PER),
        )
        for k in range(RING)
    ]
    reads = jnp.concatenate(reads, axis=0).reshape(RING, PLANE, PER)
    ids = jnp.take(reads.transpose(1, 0, 2).reshape(PLANE, RING * PER), order, axis=0)

    lists = jnp.concatenate([sources, targets], axis=0)
    ring_lists = [lists] + [along_z(lists, k) for k in range(1, RING)]

    stacked = jnp.stack(ring_lists)
    slot, target = stacked[:, 0], stacked[:, 1]
    owner = slot // PER
    core = (owner // (RING * RING)) % CORES
    dx = (owner // RING - x) % RING
    dy = (owner - y) % RING
    s = jnp.where(core == 0, dy, dx)
    f = jnp.where(core == 0, dx, dy)
    column = ((s % 2 * CORES + (core + c) % CORES) * RING + f) * PER + slot % PER
    here = owner // PLANE == z
    row_codes = jnp.where(here, s // 2 * OCT + target, -1)
    per_dir = sources.shape[1] // DIRS
    codes = [code.reshape(RING * DIRS, per_dir) for code in (row_codes, column)]

    octants = jnp.arange(OCT, dtype=jnp.int32)
    column_ids = lax.dynamic_slice_in_dim(partial_ids, device * per_owner, per_owner, 1).reshape(-1)
    selector = (octants[:, None] == column_ids[None, :]).astype(F32)
    density = jnp.dot(
        selector, received, precision=lax.Precision.HIGHEST, preferred_element_type=F32
    )

    line = [density] + [along_f(density, k) for k in range(1, RING)]
    line, codes, ids = lax.optimization_barrier((line, codes, ids))
    line = jnp.concatenate(line, axis=0)
    near1, near3 = along_s(line, 1), along_s(line, 3)
    counts, rest, flags = count(*codes)
    near1, near3, counts, rest, flags = lax.optimization_barrier(
        (near1, near3, counts, rest, flags)
    )
    low, high = along_s(near1[: 2 * OCT], 1), along_s(near3[2 * OCT :], 3)
    (rows0,) = gather((0,), ids, [line, across(line)])
    rows1, rows3 = gather((1, 3), ids, [near1, across(near1), near3, across(near3)])
    rows = (rows0, rows1, rows3)
    x = collect((0, 1, 3), counts, rows)
    low, high, x = lax.optimization_barrier((low, high, x))
    last = (flags, ids, [low, high, across(low), across(high)], x, rows, counts, kernels, rest)
    out2, out1 = finish((2, 1), *last)
    out3, out0 = finish((3, 0), *last)
    return out0 + along_z(out2, -2) + along_z(out1, -1) + along_z(out3, -3)


def solution(mesh):
    return jax.shard_map(
        body,
        mesh=mesh,
        in_specs=(P(AXES, None), P(), P(), P(AXES, None), P(AXES, None), P()),
        out_specs=P(AXES, None),
        check_vma=False,
    )
```

```python
import functools

import jax
import jax.numpy as jnp
from jax import lax
from jax.experimental import pallas as pl
from jax.experimental.pallas import tpu as pltpu
from jax.sharding import PartitionSpec as P

AXES = ("gx", "gy")
RING = 4
CORES = 2
OCT = 128
PER = 32
DIRS = 8
WIDTH = 512
PLANE = RING * RING * CORES
BLOCK = CORES * RING * PER
BF16 = jnp.bfloat16
F32 = jnp.float32
SMEM = pl.BlockSpec(memory_space=pltpu.SMEM)
VMEM = pl.BlockSpec(memory_space=pltpu.VMEM)
LIMIT = 16


def device_of(x, y, z, c):
    return ((z % RING) * CORES + c % CORES) * RING * RING + (x % RING) * RING + y % RING


def fetch(value, shift):
    pairs = []
    for z in range(RING):
        for c in range(CORES):
            for x in range(RING):
                for y in range(RING):
                    dx, dy, dz, dc = shift(c)
                    pairs.append((device_of(x + dx, y + dy, z + dz, c + dc), device_of(x, y, z, c)))
    return lax.ppermute(value, AXES, pairs)


def along_f(value, k):
    return fetch(value, lambda core: (k, 0, 0, 0) if core == 0 else (0, k, 0, 0))


def along_s(value, k):
    return fetch(value, lambda core: (0, k, 0, 0) if core == 0 else (k, 0, 0, 0))


def along_z(value, k):
    return fetch(value, lambda core: (0, 0, k, 0))


def across(value):
    return fetch(value, lambda core: (0, 0, 0, 1))


def parts(value):
    high = value.astype(BF16)
    return high, (value - high.astype(F32)).astype(BF16)


def counts_of(row_ref, col_ref, step):
    inner = row_ref.shape[1]
    rows = lax.broadcasted_iota(jnp.int32, (RING // 2 * OCT, inner), 0)
    cols = lax.broadcasted_iota(jnp.int32, (2 * BLOCK, inner), 0)
    row_hot = jnp.where(rows == row_ref[pl.ds(step, 1), :], 1.0, 0.0).astype(BF16)
    col_hot = jnp.where(cols == col_ref[pl.ds(step, 1), :], 1.0, 0.0).astype(BF16)
    counts = lax.dot_general(
        row_hot, col_hot, (((1,), (1,)), ((), ())), preferred_element_type=F32
    )
    return jnp.concatenate([counts[:OCT], counts[OCT:]], axis=1)


def count_kernel(row_ref, col_ref, out_ref, flag_ref):
    reader = pl.program_id(0)
    tops = []
    for d in range(DIRS):
        counts = counts_of(row_ref, col_ref, reader * DIRS + d)
        for s in range(RING):
            block = counts[:, s * BLOCK : (s + 1) * BLOCK]
            out_ref[s, 0, d * OCT : (d + 1) * OCT, :] = block.astype(BF16)
        tops.append(jnp.max(counts, axis=0, keepdims=True))
    large = jnp.max(functools.reduce(jnp.maximum, tops)) > 256.0
    flag_ref[reader] = large.astype(jnp.int32)


def count(row_codes, col_codes):
    codes = pl.BlockSpec(row_codes.shape, lambda k: (0, 0))
    return pl.pallas_call(
        count_kernel,
        grid=(RING,),
        in_specs=[codes, codes],
        out_specs=[pl.BlockSpec((RING, 1, DIRS * OCT, BLOCK), lambda k: (0, k, 0, 0)), SMEM],
        out_shape=[
            jax.ShapeDtypeStruct((RING, RING, DIRS * OCT, BLOCK), BF16),
            jax.ShapeDtypeStruct((RING,), jnp.int32),
        ],
        compiler_params=pltpu.CompilerParams(vmem_limit_bytes=20 << 20),
        cost_estimate=pl.CostEstimate(
            flops=100_000_000, bytes_accessed=1 << 20, transcendentals=0
        ),
        name="count",
    )(row_codes, col_codes)


def pick(ids_ref, first, refs, store):
    octants = lax.broadcasted_iota(jnp.int32, (OCT, RING * PER), 0)
    many = CORES * RING // len(refs)
    for i, ref in enumerate(refs):
        for j in range(many):
            owner = many * i + j
            table = jnp.concatenate(parts(ref[j * OCT : (j + 1) * OCT, :]), axis=1)
            hot = jnp.where(octants == ids_ref[first + owner : first + owner + 1, :], 1.0, 0.0)
            picked = lax.dot_general(
                hot.astype(BF16), table, (((0,), (0,)), ((), ())), preferred_element_type=F32
            ).astype(BF16)
            for k in range(RING):
                store(owner, k, picked[k * PER : (k + 1) * PER])


def gather_kernel(blocks, ids_ref, *refs):
    n = len(blocks)
    for i, s in enumerate(blocks):
        rows = refs[2 * n + i]

        def store(owner, k, values, rows=rows):
            rows[k, owner * PER : (owner + 1) * PER, :] = values

        pick(ids_ref, s * 2 * RING, refs[2 * i : 2 * i + 2], store)


def gather(blocks, ids, arrays):
    n = len(blocks)
    return pl.pallas_call(
        functools.partial(gather_kernel, blocks),
        in_specs=[VMEM] * (1 + 2 * n),
        out_specs=[VMEM] * n,
        out_shape=[jax.ShapeDtypeStruct((RING, BLOCK, 2 * WIDTH), BF16)] * n,
        compiler_params=pltpu.CompilerParams(vmem_limit_bytes=16 << 20),
        cost_estimate=pl.CostEstimate(
            flops=n * 1_500_000_000, bytes_accessed=n << 20, transcendentals=0
        ),
        name="gather",
    )(ids, *arrays)


def product(counts, rows):
    both = jnp.dot(
        jnp.concatenate(counts, axis=1),
        jnp.concatenate(rows, axis=0),
        preferred_element_type=F32,
    )
    return both[:, :WIDTH] + both[:, WIDTH:]


def collect_kernel(blocks, count_ref, *refs):
    rows, out_ref = refs[:-1], refs[-1]

    @pl.loop(0, RING)
    def _(k):
        for m in range(0, DIRS, 2):
            here = slice(m * OCT, (m + 2) * OCT)
            out_ref[k, here, :] = product(
                [count_ref[s, k, here, :] for s in blocks], [ref[k] for ref in rows]
            )


def collect(blocks, counts, rows):
    n = len(blocks)
    return pl.pallas_call(
        functools.partial(collect_kernel, blocks),
        in_specs=[VMEM] * (1 + n),
        out_specs=VMEM,
        out_shape=jax.ShapeDtypeStruct((RING, DIRS * OCT, WIDTH), F32),
        compiler_params=pltpu.CompilerParams(vmem_limit_bytes=8 << 20),
        cost_estimate=pl.CostEstimate(
            flops=n * 2_200_000_000, bytes_accessed=n << 20, transcendentals=0
        ),
        name="collect",
    )(counts, *rows)


def finish_kernel(
    readers, flag_ref, ids_ref, b0, b1, b2, b3, x_ref, rows0, rows1, rows3, count_ref, k_ref,
    row_ref, col_ref, out0, out1, rows2, xh, xl,
):
    def store(owner, k, values):
        rows2[k, owner * PER : (owner + 1) * PER, :] = values

    pick(ids_ref, 2 * 2 * RING, (b0, b1, b2, b3), store)
    for i, k in enumerate(readers):
        there = slice(i * OCT, (i + 1) * OCT)
        for m in range(0, DIRS, 2):
            here = slice(m * OCT, (m + 2) * OCT)
            total = x_ref[k, here, :] + product([count_ref[2, k, here, :]], [rows2[k]])
            high, low = parts(total)
            for j in range(2):
                xh[m + j, there, :] = high[j * OCT : (j + 1) * OCT]
                xl[m + j, there, :] = low[j * OCT : (j + 1) * OCT]

        @pl.when(flag_ref[k] != 0)
        def _():
            @pl.loop(0, DIRS)
            def _(d):
                exact = counts_of(row_ref, col_ref, k * DIRS + d)
                rest = (exact - exact.astype(BF16).astype(F32)).astype(BF16)
                rows = [ref[k] for ref in (rows0, rows1, rows2, rows3)]
                total = product([rest], rows)
                total += xh[d, there, :].astype(F32) + xl[d, there, :].astype(F32)
                high, low = parts(total)
                xh[d, there, :] = high
                xl[d, there, :] = low

    def dot(a, b):
        return lax.dot_general(a, b, (((1,), (1,)), ((), ())), preferred_element_type=F32)

    total = None
    for d in range(DIRS):
        high, low = parts(k_ref[d])
        term = dot(xh[d], high) + dot(xh[d], low) + dot(xl[d], high)
        total = term if total is None else total + term
    for i, out in enumerate((out0, out1)):
        out[...] = total[i * OCT : (i + 1) * OCT]


def finish(readers, flags, ids, arrays, x, rows, counts, kernels, codes):
    n = len(readers)
    return pl.pallas_call(
        functools.partial(finish_kernel, readers),
        in_specs=[SMEM] + [VMEM] * 13,
        out_specs=[VMEM] * 2,
        out_shape=[jax.ShapeDtypeStruct((OCT, WIDTH), F32)] * 2,
        scratch_shapes=[
            pltpu.VMEM((RING, BLOCK, 2 * WIDTH), BF16),
            pltpu.VMEM((DIRS, n * OCT, WIDTH), BF16),
            pltpu.VMEM((DIRS, n * OCT, WIDTH), BF16),
        ],
        compiler_params=pltpu.CompilerParams(vmem_limit_bytes=LIMIT << 20),
        cost_estimate=pl.CostEstimate(
            flops=6_000_000_000, bytes_accessed=2 << 20, transcendentals=0
        ),
        name="finish",
    )(flags, ids, *arrays, x, *rows, counts, kernels, *codes)


def body(partials, partial_ids, read_lists, sources, targets, kernels):
    gx, gy = lax.axis_index("gx"), lax.axis_index("gy")
    device = gx * (RING * RING) + gy
    z, c, x, y = gx // CORES, gx % CORES, gy // RING, gy % RING
    owners = lax.axis_size(AXES)
    per_owner = partials.shape[0] // owners

    received = lax.all_to_all(partials, AXES, split_axis=0, concat_axis=0, tiled=True)

    number = jnp.arange(PLANE, dtype=jnp.int32)
    s, w, f = number // (RING * CORES), number // RING % CORES, number % RING
    core = (w + c) % CORES
    there_x = (x + jnp.where(core == 0, f, s)) % RING
    there_y = (y + jnp.where(core == 0, s, f)) % RING
    order = core * (RING * RING) + there_x * RING + there_y
    reads = [
        lax.dynamic_slice(
            read_lists,
            (((z + k) % RING * CORES + c) * (RING * RING) + gy, z * (PLANE * PER)),
            (1, PLANE * PER),
        )
        for k in range(RING)
    ]
    reads = jnp.concatenate(reads, axis=0).reshape(RING, PLANE, PER)
    ids = jnp.take(reads.transpose(1, 0, 2).reshape(PLANE, RING * PER), order, axis=0)

    lists = jnp.concatenate([sources, targets], axis=0)
    ring_lists = [lists] + [along_z(lists, k) for k in range(1, RING)]

    stacked = jnp.stack(ring_lists)
    slot, target = stacked[:, 0], stacked[:, 1]
    owner = slot // PER
    core = (owner // (RING * RING)) % CORES
    dx = (owner // RING - x) % RING
    dy = (owner - y) % RING
    s = jnp.where(core == 0, dy, dx)
    f = jnp.where(core == 0, dx, dy)
    column = ((s % 2 * CORES + (core + c) % CORES) * RING + f) * PER + slot % PER
    here = owner // PLANE == z
    row_codes = jnp.where(here, s // 2 * OCT + target, -1)
    per_dir = sources.shape[1] // DIRS
    codes = [code.reshape(RING * DIRS, per_dir) for code in (row_codes, column)]

    octants = jnp.arange(OCT, dtype=jnp.int32)
    column_ids = lax.dynamic_slice_in_dim(partial_ids, device * per_owner, per_owner, 1).reshape(-1)
    selector = (octants[:, None] == column_ids[None, :]).astype(F32)
    density = jnp.dot(
        selector, received, precision=lax.Precision.HIGHEST, preferred_element_type=F32
    )

    line = [density] + [along_f(density, k) for k in range(1, RING)]
    line, codes, ids = lax.optimization_barrier((line, codes, ids))
    line = jnp.concatenate(line, axis=0)
    near1, near3 = along_s(line, 1), along_s(line, 3)
    counts, flags = count(*codes)
    (rows0,) = gather((0,), ids, [line, across(line)])
    near1, near3, counts, flags, rows0 = lax.optimization_barrier(
        (near1, near3, counts, flags, rows0)
    )
    low, high = along_s(near1[: 2 * OCT], 1), along_s(near3[2 * OCT :], 3)
    rows1, rows3 = gather((1, 3), ids, [near1, across(near1), near3, across(near3)])
    rows = (rows0, rows1, rows3)
    x = collect((0, 1, 3), counts, rows)
    low, high, x = lax.optimization_barrier((low, high, x))
    last = (flags, ids, [low, high, across(low), across(high)], x, rows, counts, kernels, codes)
    out2, out1 = finish((2, 1), *last)
    out3, out0 = finish((3, 0), *last)
    return out0 + along_z(out2, -2) + along_z(out1, -1) + along_z(out3, -3)


def solution(mesh):
    return jax.shard_map(
        body,
        mesh=mesh,
        in_specs=(P(AXES, None), P(), P(), P(AXES, None), P(AXES, None), P()),
        out_specs=P(AXES, None),
        check_vma=False,
    )
```

```python
import functools

import jax
import jax.numpy as jnp
from jax import lax
from jax.experimental import pallas as pl
from jax.experimental.pallas import tpu as pltpu
from jax.sharding import PartitionSpec as P

AXES = ("gx", "gy")
RING = 4
CORES = 2
OCT = 128
PER = 32
DIRS = 8
WIDTH = 512
PLANE = RING * RING * CORES
BLOCK = CORES * RING * PER
BF16 = jnp.bfloat16
F32 = jnp.float32
SMEM = pl.BlockSpec(memory_space=pltpu.SMEM)
VMEM = pl.BlockSpec(memory_space=pltpu.VMEM)
PAIR = 2
ORDER = (2, 1, 3, 0)


def device_of(x, y, z, c):
    return ((z % RING) * CORES + c % CORES) * RING * RING + (x % RING) * RING + y % RING


def fetch(value, shift):
    pairs = []
    for z in range(RING):
        for c in range(CORES):
            for x in range(RING):
                for y in range(RING):
                    dx, dy, dz, dc = shift(c)
                    pairs.append((device_of(x + dx, y + dy, z + dz, c + dc), device_of(x, y, z, c)))
    return lax.ppermute(value, AXES, pairs)


def along_f(value, k):
    return fetch(value, lambda core: (k, 0, 0, 0) if core == 0 else (0, k, 0, 0))


def along_s(value, k):
    return fetch(value, lambda core: (0, k, 0, 0) if core == 0 else (k, 0, 0, 0))


def along_z(value, k):
    return fetch(value, lambda core: (0, 0, k, 0))


def across(value):
    return fetch(value, lambda core: (0, 0, 0, 1))


def parts(value):
    high = value.astype(BF16)
    return high, (value - high.astype(F32)).astype(BF16)


def counts_of(row_ref, col_ref, step):
    inner = row_ref.shape[1]
    rows = lax.broadcasted_iota(jnp.int32, (RING // 2 * OCT, inner), 0)
    cols = lax.broadcasted_iota(jnp.int32, (2 * BLOCK, inner), 0)
    row_hot = jnp.where(rows == row_ref[pl.ds(step, 1), :], 1.0, 0.0).astype(BF16)
    col_hot = jnp.where(cols == col_ref[pl.ds(step, 1), :], 1.0, 0.0).astype(BF16)
    counts = lax.dot_general(
        row_hot, col_hot, (((1,), (1,)), ((), ())), preferred_element_type=F32
    )
    return jnp.concatenate([counts[:OCT], counts[OCT:]], axis=1)


def count_kernel(row_ref, col_ref, out_ref, flag_ref):
    reader = pl.program_id(0)
    tops = []
    for d in range(DIRS):
        counts = counts_of(row_ref, col_ref, reader * DIRS + d)
        for s in range(RING):
            block = counts[:, s * BLOCK : (s + 1) * BLOCK]
            out_ref[s, 0, d * OCT : (d + 1) * OCT, :] = block.astype(BF16)
        tops.append(jnp.max(counts, axis=0, keepdims=True))
    large = jnp.max(functools.reduce(jnp.maximum, tops)) > 256.0
    flag_ref[reader] = large.astype(jnp.int32)


def count(row_codes, col_codes):
    codes = pl.BlockSpec(row_codes.shape, lambda k: (0, 0))
    return pl.pallas_call(
        count_kernel,
        grid=(RING,),
        in_specs=[codes, codes],
        out_specs=[pl.BlockSpec((RING, 1, DIRS * OCT, BLOCK), lambda k: (0, k, 0, 0)), SMEM],
        out_shape=[
            jax.ShapeDtypeStruct((RING, RING, DIRS * OCT, BLOCK), BF16),
            jax.ShapeDtypeStruct((RING,), jnp.int32),
        ],
        compiler_params=pltpu.CompilerParams(vmem_limit_bytes=12 << 20),
        cost_estimate=pl.CostEstimate(
            flops=100_000_000, bytes_accessed=1 << 20, transcendentals=0
        ),
        name="count",
    )(row_codes, col_codes)


def pick(ids_ref, first, refs, store):
    octants = lax.broadcasted_iota(jnp.int32, (OCT, RING * PER), 0)
    many = CORES * RING // len(refs)
    for i, ref in enumerate(refs):
        for j in range(many):
            owner = many * i + j
            table = jnp.concatenate(parts(ref[j * OCT : (j + 1) * OCT, :]), axis=1)
            hot = jnp.where(octants == ids_ref[first + owner : first + owner + 1, :], 1.0, 0.0)
            picked = lax.dot_general(
                hot.astype(BF16), table, (((0,), (0,)), ((), ())), preferred_element_type=F32
            ).astype(BF16)
            for k in range(RING):
                store(owner, k, picked[k * PER : (k + 1) * PER])


def gather_kernel(blocks, ids_ref, *refs):
    n = len(blocks)
    for i, s in enumerate(blocks):
        rows = refs[2 * n + i]

        def store(owner, k, values, rows=rows):
            rows[k, owner * PER : (owner + 1) * PER, :] = values

        pick(ids_ref, s * 2 * RING, refs[2 * i : 2 * i + 2], store)


def gather(blocks, ids, arrays):
    n = len(blocks)
    return pl.pallas_call(
        functools.partial(gather_kernel, blocks),
        in_specs=[VMEM] * (1 + 2 * n),
        out_specs=[VMEM] * n,
        out_shape=[jax.ShapeDtypeStruct((RING, BLOCK, 2 * WIDTH), BF16)] * n,
        compiler_params=pltpu.CompilerParams(vmem_limit_bytes=6 << 20),
        cost_estimate=pl.CostEstimate(
            flops=n * 1_500_000_000, bytes_accessed=n << 20, transcendentals=0
        ),
        name="gather",
    )(ids, *arrays)


def product(counts, rows):
    both = jnp.dot(
        jnp.concatenate(counts, axis=1),
        jnp.concatenate(rows, axis=0),
        preferred_element_type=F32,
    )
    return both[:, :WIDTH] + both[:, WIDTH:]


def collect_kernel(blocks, first, count_ref, *refs):
    rows, out_ref = refs[:-1], refs[-1]

    @pl.loop(0, PAIR)
    def _(k):
        for m in range(0, DIRS, 2):
            here = slice(m * OCT, (m + 2) * OCT)
            out_ref[k, here, :] = product(
                [count_ref[s, first + k, here, :] for s in blocks],
                [ref[first + k] for ref in rows],
            )


def collect(blocks, first, counts, rows):
    n = len(blocks)
    return pl.pallas_call(
        functools.partial(collect_kernel, blocks, first),
        in_specs=[VMEM] * (1 + n),
        out_specs=VMEM,
        out_shape=jax.ShapeDtypeStruct((PAIR, DIRS * OCT, WIDTH), F32),
        compiler_params=pltpu.CompilerParams(vmem_limit_bytes=8 << 20),
        cost_estimate=pl.CostEstimate(
            flops=n * 1_100_000_000, bytes_accessed=n << 20, transcendentals=0
        ),
        name="collect",
    )(counts, *rows)


def finish_kernel(
    first, flag_ref, ids_ref, b0, b1, b2, b3, x_ref, rows0, rows1, rows3, count_ref, k_ref,
    row_ref, col_ref, out0, out1, rows2, xh, xl,
):
    def store(owner, k, values):
        rows2[k, owner * PER : (owner + 1) * PER, :] = values

    pick(ids_ref, 2 * 2 * RING, (b0, b1, b2, b3), store)
    for i in range(PAIR):
        k = first + i
        there = slice(i * OCT, (i + 1) * OCT)
        for m in range(0, DIRS, 2):
            here = slice(m * OCT, (m + 2) * OCT)
            total = x_ref[i, here, :] + product([count_ref[2, k, here, :]], [rows2[k]])
            high, low = parts(total)
            for j in range(2):
                xh[m + j, there, :] = high[j * OCT : (j + 1) * OCT]
                xl[m + j, there, :] = low[j * OCT : (j + 1) * OCT]

        @pl.when(flag_ref[k] != 0)
        def _():
            @pl.loop(0, DIRS)
            def _(d):
                exact = counts_of(row_ref, col_ref, k * DIRS + d)
                rest = (exact - exact.astype(BF16).astype(F32)).astype(BF16)
                rows = [ref[k] for ref in (rows0, rows1, rows2, rows3)]
                total = product([rest], rows)
                total += xh[d, there, :].astype(F32) + xl[d, there, :].astype(F32)
                high, low = parts(total)
                xh[d, there, :] = high
                xl[d, there, :] = low

    def dot(a, b):
        return lax.dot_general(a, b, (((1,), (1,)), ((), ())), preferred_element_type=F32)

    total = None
    for d in range(DIRS):
        high, low = parts(k_ref[d])
        term = dot(xh[d], high) + dot(xh[d], low) + dot(xl[d], high)
        total = term if total is None else total + term
    for i, out in enumerate((out0, out1)):
        out[...] = total[i * OCT : (i + 1) * OCT]


def finish(first, flags, ids, arrays, x, rows, counts, kernels, codes):
    return pl.pallas_call(
        functools.partial(finish_kernel, first),
        in_specs=[SMEM] + [VMEM] * 13,
        out_specs=[VMEM] * 2,
        out_shape=[jax.ShapeDtypeStruct((OCT, WIDTH), F32)] * 2,
        scratch_shapes=[
            pltpu.VMEM((RING, BLOCK, 2 * WIDTH), BF16),
            pltpu.VMEM((DIRS, PAIR * OCT, WIDTH), BF16),
            pltpu.VMEM((DIRS, PAIR * OCT, WIDTH), BF16),
        ],
        compiler_params=pltpu.CompilerParams(vmem_limit_bytes=12 << 20),
        cost_estimate=pl.CostEstimate(
            flops=6_000_000_000, bytes_accessed=2 << 20, transcendentals=0
        ),
        name="finish",
    )(flags, ids, *arrays, x, *rows, counts, kernels, *codes)


def body(partials, partial_ids, read_lists, sources, targets, kernels):
    gx, gy = lax.axis_index("gx"), lax.axis_index("gy")
    device = gx * (RING * RING) + gy
    z, c, x, y = gx // CORES, gx % CORES, gy // RING, gy % RING
    owners = lax.axis_size(AXES)
    per_owner = partials.shape[0] // owners

    received = lax.all_to_all(partials, AXES, split_axis=0, concat_axis=0, tiled=True)

    number = jnp.arange(PLANE, dtype=jnp.int32)
    s, w, f = number // (RING * CORES), number // RING % CORES, number % RING
    core = (w + c) % CORES
    there_x = (x + jnp.where(core == 0, f, s)) % RING
    there_y = (y + jnp.where(core == 0, s, f)) % RING
    order = core * (RING * RING) + there_x * RING + there_y
    reads = [
        lax.dynamic_slice(
            read_lists,
            (((z + k) % RING * CORES + c) * (RING * RING) + gy, z * (PLANE * PER)),
            (1, PLANE * PER),
        )
        for k in ORDER
    ]
    reads = jnp.concatenate(reads, axis=0).reshape(RING, PLANE, PER)
    ids = jnp.take(reads.transpose(1, 0, 2).reshape(PLANE, RING * PER), order, axis=0)

    lists = jnp.concatenate([sources, targets], axis=0)
    ring_lists = {0: lists, **{k: along_z(lists, k) for k in range(1, RING)}}

    stacked = jnp.stack([ring_lists[k] for k in ORDER])
    slot, target = stacked[:, 0], stacked[:, 1]
    owner = slot // PER
    core = (owner // (RING * RING)) % CORES
    dx = (owner // RING - x) % RING
    dy = (owner - y) % RING
    s = jnp.where(core == 0, dy, dx)
    f = jnp.where(core == 0, dx, dy)
    column = ((s % 2 * CORES + (core + c) % CORES) * RING + f) * PER + slot % PER
    here = owner // PLANE == z
    row_codes = jnp.where(here, s // 2 * OCT + target, -1)
    per_dir = sources.shape[1] // DIRS
    codes = [code.reshape(RING * DIRS, per_dir) for code in (row_codes, column)]

    octants = jnp.arange(OCT, dtype=jnp.int32)
    column_ids = lax.dynamic_slice_in_dim(partial_ids, device * per_owner, per_owner, 1).reshape(-1)
    selector = (octants[:, None] == column_ids[None, :]).astype(F32)
    density = jnp.dot(
        selector, received, precision=lax.Precision.HIGHEST, preferred_element_type=F32
    )

    line = [density] + [along_f(density, k) for k in range(1, RING)]
    line, codes, ids = lax.optimization_barrier((line, codes, ids))
    line = jnp.concatenate(line, axis=0)
    near1, near3 = along_s(line, 1), along_s(line, 3)
    counts, flags = count(*codes)
    near1, near3, counts, flags = lax.optimization_barrier((near1, near3, counts, flags))
    low, high = along_s(near1[: 2 * OCT], 1), along_s(near3[2 * OCT :], 3)
    (rows0,) = gather((0,), ids, [line, across(line)])
    rows1, rows3 = gather((1, 3), ids, [near1, across(near1), near3, across(near3)])
    rows = (rows0, rows1, rows3)
    x = [collect((0, 1, 3), 0, counts, rows), None]
    low, high, x[0], rows = lax.optimization_barrier((low, high, x[0], rows))
    far = [low, high, across(low), across(high)]
    x[1] = collect((0, 1, 3), PAIR, counts, rows)
    last = (rows, counts, kernels, codes)
    out2, out1 = finish(0, flags, ids, far, x[0], *last)
    ring2, ring1 = along_z(out2, -2), along_z(out1, -1)
    out3, out0 = finish(PAIR, flags, ids, far, x[1], *last)
    ring3 = along_z(out3, -3)
    return out0 + ring3 + ring2 + ring1


def solution(mesh):
    return jax.shard_map(
        body,
        mesh=mesh,
        in_specs=(P(AXES, None), P(), P(), P(AXES, None), P(AXES, None), P()),
        out_specs=P(AXES, None),
        check_vma=False,
    )
```

```python
import functools

import jax
import jax.numpy as jnp
from jax import lax
from jax.experimental import pallas as pl
from jax.experimental.pallas import tpu as pltpu
from jax.sharding import PartitionSpec as P

AXES = ("gx", "gy")
RING = 4
CORES = 2
OCT = 128
PER = 32
DIRS = 8
WIDTH = 512
PLANE = RING * RING * CORES
BLOCK = CORES * RING * PER
BF16 = jnp.bfloat16
F32 = jnp.float32
SMEM = pl.BlockSpec(memory_space=pltpu.SMEM)
VMEM = pl.BlockSpec(memory_space=pltpu.VMEM)
PAIR = 2
ORDER = (2, 1, 3, 0)


def device_of(x, y, z, c):
    return ((z % RING) * CORES + c % CORES) * RING * RING + (x % RING) * RING + y % RING


def fetch(value, shift):
    pairs = []
    for z in range(RING):
        for c in range(CORES):
            for x in range(RING):
                for y in range(RING):
                    dx, dy, dz, dc = shift(c)
                    pairs.append((device_of(x + dx, y + dy, z + dz, c + dc), device_of(x, y, z, c)))
    return lax.ppermute(value, AXES, pairs)


def along_f(value, k):
    return fetch(value, lambda core: (k, 0, 0, 0) if core == 0 else (0, k, 0, 0))


def along_s(value, k):
    return fetch(value, lambda core: (0, k, 0, 0) if core == 0 else (k, 0, 0, 0))


def along_z(value, k):
    return fetch(value, lambda core: (0, 0, k, 0))


def across(value):
    return fetch(value, lambda core: (0, 0, 0, 1))


def parts(value):
    high = value.astype(BF16)
    return high, (value - high.astype(F32)).astype(BF16)


def counts_of(row_ref, col_ref, step):
    inner = row_ref.shape[1]
    rows = lax.broadcasted_iota(jnp.int32, (RING // 2 * OCT, inner), 0)
    cols = lax.broadcasted_iota(jnp.int32, (2 * BLOCK, inner), 0)
    row_hot = jnp.where(rows == row_ref[pl.ds(step, 1), :], 1.0, 0.0).astype(BF16)
    col_hot = jnp.where(cols == col_ref[pl.ds(step, 1), :], 1.0, 0.0).astype(BF16)
    counts = lax.dot_general(
        row_hot, col_hot, (((1,), (1,)), ((), ())), preferred_element_type=F32
    )
    return jnp.concatenate([counts[:OCT], counts[OCT:]], axis=1)


def count_kernel(row_ref, col_ref, out_ref, flag_ref):
    reader = pl.program_id(0)
    tops = []
    for d in range(DIRS):
        counts = counts_of(row_ref, col_ref, reader * DIRS + d)
        for s in range(RING):
            block = counts[:, s * BLOCK : (s + 1) * BLOCK]
            out_ref[s, 0, d * OCT : (d + 1) * OCT, :] = block.astype(BF16)
        tops.append(jnp.max(counts, axis=0, keepdims=True))
    large = jnp.max(functools.reduce(jnp.maximum, tops)) > 256.0
    flag_ref[reader] = large.astype(jnp.int32)


def count(row_codes, col_codes):
    codes = pl.BlockSpec(row_codes.shape, lambda k: (0, 0))
    return pl.pallas_call(
        count_kernel,
        grid=(RING,),
        in_specs=[codes, codes],
        out_specs=[pl.BlockSpec((RING, 1, DIRS * OCT, BLOCK), lambda k: (0, k, 0, 0)), SMEM],
        out_shape=[
            jax.ShapeDtypeStruct((RING, RING, DIRS * OCT, BLOCK), BF16),
            jax.ShapeDtypeStruct((RING,), jnp.int32),
        ],
        compiler_params=pltpu.CompilerParams(vmem_limit_bytes=12 << 20),
        cost_estimate=pl.CostEstimate(
            flops=100_000_000, bytes_accessed=1 << 20, transcendentals=0
        ),
        name="count",
    )(row_codes, col_codes)


def pick(ids_ref, first, refs, store):
    octants = lax.broadcasted_iota(jnp.int32, (OCT, RING * PER), 0)
    many = CORES * RING // len(refs)
    for i, ref in enumerate(refs):
        for j in range(many):
            owner = many * i + j
            table = jnp.concatenate(parts(ref[j * OCT : (j + 1) * OCT, :]), axis=1)
            hot = jnp.where(octants == ids_ref[first + owner : first + owner + 1, :], 1.0, 0.0)
            picked = lax.dot_general(
                hot.astype(BF16), table, (((0,), (0,)), ((), ())), preferred_element_type=F32
            ).astype(BF16)
            for k in range(RING):
                store(owner, k, picked[k * PER : (k + 1) * PER])


def gather_kernel(blocks, ids_ref, *refs):
    n = len(blocks)
    per = len(refs) // n - 1
    for i, s in enumerate(blocks):
        rows = refs[per * n + i]

        def store(owner, k, values, rows=rows):
            rows[k, owner * PER : (owner + 1) * PER, :] = values

        pick(ids_ref, s * 2 * RING, refs[per * i : per * (i + 1)], store)


def gather(blocks, ids, arrays):
    n = len(blocks)
    return pl.pallas_call(
        functools.partial(gather_kernel, blocks),
        in_specs=[VMEM] * (1 + len(arrays)),
        out_specs=[VMEM] * n,
        out_shape=[jax.ShapeDtypeStruct((RING, BLOCK, 2 * WIDTH), BF16)] * n,
        compiler_params=pltpu.CompilerParams(vmem_limit_bytes=6 << 20),
        cost_estimate=pl.CostEstimate(
            flops=n * 1_500_000_000, bytes_accessed=n << 20, transcendentals=0
        ),
        name="gather",
    )(ids, *arrays)


def product(counts, rows):
    both = jnp.dot(
        jnp.concatenate(counts, axis=1),
        jnp.concatenate(rows, axis=0),
        preferred_element_type=F32,
    )
    return both[:, :WIDTH] + both[:, WIDTH:]


def collect_kernel(blocks, first, count_ref, *refs):
    rows, out_ref = refs[:-1], refs[-1]

    @pl.loop(0, PAIR)
    def _(k):
        for m in range(0, DIRS, 2):
            here = slice(m * OCT, (m + 2) * OCT)
            out_ref[k, here, :] = product(
                [count_ref[s, first + k, here, :] for s in blocks],
                [ref[first + k] for ref in rows],
            )


def collect(blocks, first, counts, rows):
    n = len(blocks)
    return pl.pallas_call(
        functools.partial(collect_kernel, blocks, first),
        in_specs=[VMEM] * (1 + n),
        out_specs=VMEM,
        out_shape=jax.ShapeDtypeStruct((PAIR, DIRS * OCT, WIDTH), F32),
        compiler_params=pltpu.CompilerParams(vmem_limit_bytes=8 << 20),
        cost_estimate=pl.CostEstimate(
            flops=n * 1_100_000_000, bytes_accessed=n << 20, transcendentals=0
        ),
        name="collect",
    )(counts, *rows)


def finish_kernel(
    first, skip, flag_ref, x_ref, rows0, rows1, rows2, rows3, count_ref, k_ref, row_ref, col_ref,
    *refs,
):
    outs, xh, xl = refs[:-2], refs[-2], refs[-1]
    for i in range(len(outs)):
        k = first + i
        there = slice(i * OCT, (i + 1) * OCT)
        for m in range(0, DIRS, 2):
            here = slice(m * OCT, (m + 2) * OCT)
            total = x_ref[skip + i, here, :] + product([count_ref[2, k, here, :]], [rows2[k]])
            high, low = parts(total)
            for j in range(2):
                xh[m + j, there, :] = high[j * OCT : (j + 1) * OCT]
                xl[m + j, there, :] = low[j * OCT : (j + 1) * OCT]

        @pl.when(flag_ref[k] != 0)
        def _():
            @pl.loop(0, DIRS)
            def _(d):
                exact = counts_of(row_ref, col_ref, k * DIRS + d)
                rest = (exact - exact.astype(BF16).astype(F32)).astype(BF16)
                rows = [ref[k] for ref in (rows0, rows1, rows2, rows3)]
                total = product([rest], rows)
                total += xh[d, there, :].astype(F32) + xl[d, there, :].astype(F32)
                high, low = parts(total)
                xh[d, there, :] = high
                xl[d, there, :] = low

    def dot(a, b):
        return lax.dot_general(a, b, (((1,), (1,)), ((), ())), preferred_element_type=F32)

    total = None
    for d in range(DIRS):
        high, low = parts(k_ref[d])
        term = dot(xh[d], high) + dot(xh[d], low) + dot(xl[d], high)
        total = term if total is None else total + term
    for i, out in enumerate(outs):
        out[...] = total[i * OCT : (i + 1) * OCT]


def finish(first, n, flags, x, rows, counts, kernels, codes):
    return pl.pallas_call(
        functools.partial(finish_kernel, first, first % PAIR),
        in_specs=[SMEM] + [VMEM] * 9,
        out_specs=[VMEM] * n,
        out_shape=[jax.ShapeDtypeStruct((OCT, WIDTH), F32)] * n,
        scratch_shapes=[pltpu.VMEM((DIRS, n * OCT, WIDTH), BF16)] * 2,
        compiler_params=pltpu.CompilerParams(vmem_limit_bytes=10 << 20),
        cost_estimate=pl.CostEstimate(
            flops=n * 3_000_000_000, bytes_accessed=2 << 20, transcendentals=0
        ),
        name="finish",
    )(flags, x, *rows, counts, kernels, *codes)


def body(partials, partial_ids, read_lists, sources, targets, kernels):
    gx, gy = lax.axis_index("gx"), lax.axis_index("gy")
    device = gx * (RING * RING) + gy
    z, c, x, y = gx // CORES, gx % CORES, gy // RING, gy % RING
    owners = lax.axis_size(AXES)
    per_owner = partials.shape[0] // owners

    received = lax.all_to_all(partials, AXES, split_axis=0, concat_axis=0, tiled=True)

    number = jnp.arange(PLANE, dtype=jnp.int32)
    s, w, f = number // (RING * CORES), number // RING % CORES, number % RING
    core = (w + c) % CORES
    there_x = (x + jnp.where(core == 0, f, s)) % RING
    there_y = (y + jnp.where(core == 0, s, f)) % RING
    order = core * (RING * RING) + there_x * RING + there_y
    reads = [
        lax.dynamic_slice(
            read_lists,
            (((z + k) % RING * CORES + c) * (RING * RING) + gy, z * (PLANE * PER)),
            (1, PLANE * PER),
        )
        for k in ORDER
    ]
    reads = jnp.concatenate(reads, axis=0).reshape(RING, PLANE, PER)
    ids = jnp.take(reads.transpose(1, 0, 2).reshape(PLANE, RING * PER), order, axis=0)

    lists = jnp.concatenate([sources, targets], axis=0)
    ring_lists = {0: lists, **{k: along_z(lists, k) for k in range(1, RING)}}

    stacked = jnp.stack([ring_lists[k] for k in ORDER])
    slot, target = stacked[:, 0], stacked[:, 1]
    owner = slot // PER
    core = (owner // (RING * RING)) % CORES
    dx = (owner // RING - x) % RING
    dy = (owner - y) % RING
    s = jnp.where(core == 0, dy, dx)
    f = jnp.where(core == 0, dx, dy)
    column = ((s % 2 * CORES + (core + c) % CORES) * RING + f) * PER + slot % PER
    here = owner // PLANE == z
    row_codes = jnp.where(here, s // 2 * OCT + target, -1)
    per_dir = sources.shape[1] // DIRS
    codes = [code.reshape(RING * DIRS, per_dir) for code in (row_codes, column)]

    octants = jnp.arange(OCT, dtype=jnp.int32)
    column_ids = lax.dynamic_slice_in_dim(partial_ids, device * per_owner, per_owner, 1).reshape(-1)
    selector = (octants[:, None] == column_ids[None, :]).astype(F32)
    density = jnp.dot(
        selector, received, precision=lax.Precision.HIGHEST, preferred_element_type=F32
    )

    line = [density] + [along_f(density, k) for k in range(1, RING)]
    line, codes, ids = lax.optimization_barrier((line, codes, ids))
    line = jnp.concatenate(line, axis=0)
    near1, near3 = along_s(line, 1), along_s(line, 3)
    counts, flags = count(*codes)
    near1, near3, counts, flags = lax.optimization_barrier((near1, near3, counts, flags))
    low, high = along_s(near1[: 2 * OCT], 1), along_s(near3[2 * OCT :], 3)
    (rows0,) = gather((0,), ids, [line, across(line)])
    rows1, rows3 = gather((1, 3), ids, [near1, across(near1), near3, across(near3)])
    rows = (rows0, rows1, rows3)
    x = [collect((0, 1, 3), 0, counts, rows), None]
    low, high, x[0], rows = lax.optimization_barrier((low, high, x[0], rows))
    far = [low, high, across(low), across(high)]
    x[1] = collect((0, 1, 3), PAIR, counts, rows)
    (rows2,) = gather((2,), ids, far)
    last = (rows[:2] + (rows2,) + rows[2:], counts, kernels, codes)
    out2, out1 = finish(0, 2, flags, x[0], *last)
    ring2, ring1 = along_z(out2, -2), along_z(out1, -1)
    (out3,) = finish(2, 1, flags, x[1], *last)
    ring3 = along_z(out3, -3)
    (out0,) = finish(3, 1, flags, x[1], *last)
    return out0 + ring3 + ring2 + ring1


def solution(mesh):
    return jax.shard_map(
        body,
        mesh=mesh,
        in_specs=(P(AXES, None), P(), P(), P(AXES, None), P(AXES, None), P()),
        out_specs=P(AXES, None),
        check_vma=False,
    )
```

```python
import functools

import jax
import jax.numpy as jnp
from jax import lax
from jax.experimental import pallas as pl
from jax.experimental.pallas import tpu as pltpu
from jax.sharding import PartitionSpec as P

AXES = ("gx", "gy")
RING = 4
CORES = 2
OCT = 128
PER = 32
DIRS = 8
WIDTH = 512
PLANE = RING * RING * CORES
BLOCK = CORES * RING * PER
BF16 = jnp.bfloat16
F32 = jnp.float32
SMEM = pl.BlockSpec(memory_space=pltpu.SMEM)
VMEM = pl.BlockSpec(memory_space=pltpu.VMEM)
PAIR = 2
ORDER = (2, 1, 3, 0)


def device_of(x, y, z, c):
    return ((z % RING) * CORES + c % CORES) * RING * RING + (x % RING) * RING + y % RING


def fetch(value, shift):
    pairs = []
    for z in range(RING):
        for c in range(CORES):
            for x in range(RING):
                for y in range(RING):
                    dx, dy, dz, dc = shift(c)
                    pairs.append((device_of(x + dx, y + dy, z + dz, c + dc), device_of(x, y, z, c)))
    return lax.ppermute(value, AXES, pairs)


def along_f(value, k):
    return fetch(value, lambda core: (k, 0, 0, 0) if core == 0 else (0, k, 0, 0))


def along_s(value, k):
    return fetch(value, lambda core: (0, k, 0, 0) if core == 0 else (k, 0, 0, 0))


def along_z(value, k):
    return fetch(value, lambda core: (0, 0, k, 0))


def across(value):
    return fetch(value, lambda core: (0, 0, 0, 1))


def parts(value):
    high = value.astype(BF16)
    return high, (value - high.astype(F32)).astype(BF16)


def counts_of(row_ref, col_ref, step):
    inner = row_ref.shape[1]
    rows = lax.broadcasted_iota(jnp.int32, (RING // 2 * OCT, inner), 0)
    cols = lax.broadcasted_iota(jnp.int32, (2 * BLOCK, inner), 0)
    row_hot = jnp.where(rows == row_ref[pl.ds(step, 1), :], 1.0, 0.0).astype(BF16)
    col_hot = jnp.where(cols == col_ref[pl.ds(step, 1), :], 1.0, 0.0).astype(BF16)
    counts = lax.dot_general(
        row_hot, col_hot, (((1,), (1,)), ((), ())), preferred_element_type=F32
    )
    return jnp.concatenate([counts[:OCT], counts[OCT:]], axis=1)


def count_kernel(row_ref, col_ref, out_ref, flag_ref):
    reader = pl.program_id(0)
    tops = []
    for d in range(DIRS):
        counts = counts_of(row_ref, col_ref, reader * DIRS + d)
        for s in range(RING):
            block = counts[:, s * BLOCK : (s + 1) * BLOCK]
            out_ref[s, 0, d * OCT : (d + 1) * OCT, :] = block.astype(BF16)
        tops.append(jnp.max(counts, axis=0, keepdims=True))
    large = jnp.max(functools.reduce(jnp.maximum, tops)) > 256.0
    flag_ref[reader] = large.astype(jnp.int32)


def count(row_codes, col_codes):
    codes = pl.BlockSpec(row_codes.shape, lambda k: (0, 0))
    return pl.pallas_call(
        count_kernel,
        grid=(RING,),
        in_specs=[codes, codes],
        out_specs=[pl.BlockSpec((RING, 1, DIRS * OCT, BLOCK), lambda k: (0, k, 0, 0)), SMEM],
        out_shape=[
            jax.ShapeDtypeStruct((RING, RING, DIRS * OCT, BLOCK), BF16),
            jax.ShapeDtypeStruct((RING,), jnp.int32),
        ],
        compiler_params=pltpu.CompilerParams(vmem_limit_bytes=12 << 20),
        cost_estimate=pl.CostEstimate(
            flops=100_000_000, bytes_accessed=1 << 20, transcendentals=0
        ),
        name="count",
    )(row_codes, col_codes)


def pick(ids_ref, first, refs, store):
    octants = lax.broadcasted_iota(jnp.int32, (OCT, RING * PER), 0)
    many = CORES * RING // len(refs)
    for i, ref in enumerate(refs):
        for j in range(many):
            owner = many * i + j
            table = jnp.concatenate(parts(ref[j * OCT : (j + 1) * OCT, :]), axis=1)
            hot = jnp.where(octants == ids_ref[first + owner : first + owner + 1, :], 1.0, 0.0)
            picked = lax.dot_general(
                hot.astype(BF16), table, (((0,), (0,)), ((), ())), preferred_element_type=F32
            ).astype(BF16)
            for k in range(RING):
                store(owner, k, picked[k * PER : (k + 1) * PER])


def gather_kernel(blocks, ids_ref, *refs):
    n = len(blocks)
    per = len(refs) // n - 1
    for i, s in enumerate(blocks):
        rows = refs[per * n + i]

        def store(owner, k, values, rows=rows):
            rows[k, owner * PER : (owner + 1) * PER, :] = values

        pick(ids_ref, s * 2 * RING, refs[per * i : per * (i + 1)], store)


def gather(blocks, ids, arrays):
    n = len(blocks)
    return pl.pallas_call(
        functools.partial(gather_kernel, blocks),
        in_specs=[VMEM] * (1 + len(arrays)),
        out_specs=[VMEM] * n,
        out_shape=[jax.ShapeDtypeStruct((RING, BLOCK, 2 * WIDTH), BF16)] * n,
        compiler_params=pltpu.CompilerParams(vmem_limit_bytes=6 << 20),
        cost_estimate=pl.CostEstimate(
            flops=n * 1_500_000_000, bytes_accessed=n << 20, transcendentals=0
        ),
        name="gather",
    )(ids, *arrays)


def product(counts, rows):
    both = jnp.dot(
        jnp.concatenate(counts, axis=1),
        jnp.concatenate(rows, axis=0),
        preferred_element_type=F32,
    )
    return both[:, :WIDTH] + both[:, WIDTH:]


def collect_kernel(blocks, first, count_ref, *refs):
    rows, out_ref = refs[:-1], refs[-1]

    @pl.loop(0, PAIR)
    def _(k):
        for m in range(0, DIRS, 2):
            here = slice(m * OCT, (m + 2) * OCT)
            out_ref[k, here, :] = product(
                [count_ref[s, first + k, here, :] for s in blocks],
                [ref[first + k] for ref in rows],
            )


def collect(blocks, first, counts, rows):
    n = len(blocks)
    return pl.pallas_call(
        functools.partial(collect_kernel, blocks, first),
        in_specs=[VMEM] * (1 + n),
        out_specs=VMEM,
        out_shape=jax.ShapeDtypeStruct((PAIR, DIRS * OCT, WIDTH), F32),
        compiler_params=pltpu.CompilerParams(vmem_limit_bytes=8 << 20),
        cost_estimate=pl.CostEstimate(
            flops=n * 1_100_000_000, bytes_accessed=n << 20, transcendentals=0
        ),
        name="collect",
    )(counts, *rows)


def finish_kernel(
    first, flag_ref, x_ref, rows0, rows1, rows2, rows3, count_ref, kh_ref, kl_ref,
    row_ref, col_ref, *refs,
):
    outs, xh, xl = refs[:-2], refs[-2], refs[-1]
    for i in range(len(outs)):
        k = first + i
        there = slice(i * OCT, (i + 1) * OCT)
        for m in range(0, DIRS, 2):
            here = slice(m * OCT, (m + 2) * OCT)
            old = x_ref[k % PAIR, here, :]
            total = old + product([count_ref[2, k, here, :]], [rows2[k]])
            high, low = parts(total)
            for j in range(2):
                xh[m + j, there, :] = high[j * OCT : (j + 1) * OCT]
                xl[m + j, there, :] = low[j * OCT : (j + 1) * OCT]

        @pl.when(flag_ref[k] != 0)
        def _():
            @pl.loop(0, DIRS)
            def _(d):
                exact = counts_of(row_ref, col_ref, k * DIRS + d)
                rest = (exact - exact.astype(BF16).astype(F32)).astype(BF16)
                rows = [ref[k] for ref in (rows0, rows1, rows2, rows3)]
                total = product([rest], rows)
                total += xh[d, there, :].astype(F32) + xl[d, there, :].astype(F32)
                high, low = parts(total)
                xh[d, there, :] = high
                xl[d, there, :] = low

    def dot(a, b):
        return jnp.dot(a, b, preferred_element_type=F32)

    total = None
    for d in range(DIRS):
        term = dot(xh[d], kh_ref[d]) + dot(xh[d], kl_ref[d]) + dot(xl[d], kh_ref[d])
        total = term if total is None else total + term
    for i, out in enumerate(outs):
        out[...] = total[i * OCT : (i + 1) * OCT]


def finish(first, n, flags, x, rows, counts, kernels, codes):
    return pl.pallas_call(
        functools.partial(finish_kernel, first),
        in_specs=[SMEM] + [VMEM] * 10,
        out_specs=[VMEM] * n,
        out_shape=[jax.ShapeDtypeStruct((OCT, WIDTH), F32)] * n,
        scratch_shapes=[pltpu.VMEM((DIRS, n * OCT, WIDTH), BF16)] * 2,
        compiler_params=pltpu.CompilerParams(vmem_limit_bytes=10 << 20),
        cost_estimate=pl.CostEstimate(
            flops=n * 3_000_000_000, bytes_accessed=2 << 20, transcendentals=0
        ),
        name="finish",
    )(flags, x, *rows, counts, *kernels, *codes)


def turn_kernel(k_ref, high_ref, low_ref):
    high_ref[0], low_ref[0] = parts(k_ref[0].T)


def turn(kernels):
    spec = pl.BlockSpec((1, WIDTH, WIDTH), lambda d: (d, 0, 0))
    return pl.pallas_call(
        turn_kernel,
        grid=(DIRS,),
        in_specs=[spec],
        out_specs=[spec] * 2,
        out_shape=[jax.ShapeDtypeStruct(kernels.shape, BF16)] * 2,
        compiler_params=pltpu.CompilerParams(vmem_limit_bytes=12 << 20),
        cost_estimate=pl.CostEstimate(
            flops=100_000_000, bytes_accessed=1 << 20, transcendentals=0
        ),
        name="turn",
    )(kernels)


def body(partials, partial_ids, read_lists, sources, targets, kernels):
    gx, gy = lax.axis_index("gx"), lax.axis_index("gy")
    device = gx * (RING * RING) + gy
    z, c, x, y = gx // CORES, gx % CORES, gy // RING, gy % RING
    owners = lax.axis_size(AXES)
    per_owner = partials.shape[0] // owners

    received = lax.all_to_all(partials, AXES, split_axis=0, concat_axis=0, tiled=True)

    number = jnp.arange(PLANE, dtype=jnp.int32)
    s, w, f = number // (RING * CORES), number // RING % CORES, number % RING
    core = (w + c) % CORES
    there_x = (x + jnp.where(core == 0, f, s)) % RING
    there_y = (y + jnp.where(core == 0, s, f)) % RING
    order = core * (RING * RING) + there_x * RING + there_y
    reads = [
        lax.dynamic_slice(
            read_lists,
            (((z + k) % RING * CORES + c) * (RING * RING) + gy, z * (PLANE * PER)),
            (1, PLANE * PER),
        )
        for k in ORDER
    ]
    reads = jnp.concatenate(reads, axis=0).reshape(RING, PLANE, PER)
    ids = jnp.take(reads.transpose(1, 0, 2).reshape(PLANE, RING * PER), order, axis=0)

    lists = jnp.concatenate([sources, targets], axis=0)
    ring_lists = {0: lists, **{k: along_z(lists, k) for k in range(1, RING)}}

    stacked = jnp.stack([ring_lists[k] for k in ORDER])
    slot, target = stacked[:, 0], stacked[:, 1]
    owner = slot // PER
    core = (owner // (RING * RING)) % CORES
    dx = (owner // RING - x) % RING
    dy = (owner - y) % RING
    s = jnp.where(core == 0, dy, dx)
    f = jnp.where(core == 0, dx, dy)
    column = ((s % 2 * CORES + (core + c) % CORES) * RING + f) * PER + slot % PER
    here = owner // PLANE == z
    row_codes = jnp.where(here, s // 2 * OCT + target, -1)
    per_dir = sources.shape[1] // DIRS
    codes = [code.reshape(RING * DIRS, per_dir) for code in (row_codes, column)]

    received, *kernels = lax.optimization_barrier((received, *turn(kernels)))
    octants = jnp.arange(OCT, dtype=jnp.int32)
    column_ids = lax.dynamic_slice_in_dim(partial_ids, device * per_owner, per_owner, 1).reshape(-1)
    selector = (octants[:, None] == column_ids[None, :]).astype(F32)
    density = jnp.dot(
        selector, received, precision=lax.Precision.HIGHEST, preferred_element_type=F32
    )

    line = [density] + [along_f(density, k) for k in range(1, RING)]
    line, codes, ids = lax.optimization_barrier((line, codes, ids))
    line = jnp.concatenate(line, axis=0)
    near1, near3 = along_s(line, 1), along_s(line, 3)
    counts, flags = count(*codes)
    near1, near3, counts, flags = lax.optimization_barrier((near1, near3, counts, flags))
    low, high = along_s(near1[: 2 * OCT], 1), along_s(near3[2 * OCT :], 3)
    (rows0,) = gather((0,), ids, [line, across(line)])
    rows1, rows3 = gather((1, 3), ids, [near1, across(near1), near3, across(near3)])
    rows = (rows0, rows1, rows3)
    x = [collect((0, 1, 3), 0, counts, rows), None]
    low, high, x[0], rows = lax.optimization_barrier((low, high, x[0], rows))
    far = [low, high, across(low), across(high)]
    x[1] = collect((0, 1, 3), PAIR, counts, rows)
    (rows2,) = gather((2,), ids, far)
    last = (rows[:2] + (rows2,) + rows[2:], counts, kernels, codes)
    out2, out1 = finish(0, 2, flags, x[0], *last)
    ring2, ring1 = along_z(out2, -2), along_z(out1, -1)
    (out3,) = finish(2, 1, flags, x[1], *last)
    ring3 = along_z(out3, -3)
    (out0,) = finish(3, 1, flags, x[1], *last)
    return out0 + ring3 + ring2 + ring1


def solution(mesh):
    return jax.shard_map(
        body,
        mesh=mesh,
        in_specs=(P(AXES, None), P(), P(), P(AXES, None), P(AXES, None), P()),
        out_specs=P(AXES, None),
        check_vma=False,
    )
```

```python
import functools

import jax
import jax.numpy as jnp
from jax import lax
from jax.experimental import pallas as pl
from jax.experimental.pallas import tpu as pltpu
from jax.sharding import PartitionSpec as P

AXES = ("gx", "gy")
RING = 4
CORES = 2
OCT = 128
PER = 32
DIRS = 8
WIDTH = 512
PLANE = RING * RING * CORES
BLOCK = CORES * RING * PER
BF16 = jnp.bfloat16
F32 = jnp.float32
SMEM = pl.BlockSpec(memory_space=pltpu.SMEM)
VMEM = pl.BlockSpec(memory_space=pltpu.VMEM)
PAIR = 2
ORDER = (2, 0, 1, 3)


def device_of(x, y, z, c):
    return ((z % RING) * CORES + c % CORES) * RING * RING + (x % RING) * RING + y % RING


def fetch(value, shift):
    pairs = []
    for z in range(RING):
        for c in range(CORES):
            for x in range(RING):
                for y in range(RING):
                    dx, dy, dz, dc = shift(c)
                    pairs.append((device_of(x + dx, y + dy, z + dz, c + dc), device_of(x, y, z, c)))
    return lax.ppermute(value, AXES, pairs)


def along_f(value, k):
    return fetch(value, lambda core: (k, 0, 0, 0) if core == 0 else (0, k, 0, 0))


def along_s(value, k):
    return fetch(value, lambda core: (0, k, 0, 0) if core == 0 else (k, 0, 0, 0))


def along_z(value, k):
    return fetch(value, lambda core: (0, 0, k, 0))


def across(value):
    return fetch(value, lambda core: (0, 0, 0, 1))


def parts(value):
    high = value.astype(BF16)
    return high, (value - high.astype(F32)).astype(BF16)


def counts_of(row_ref, col_ref, step):
    inner = row_ref.shape[1]
    rows = lax.broadcasted_iota(jnp.int32, (RING // 2 * OCT, inner), 0)
    cols = lax.broadcasted_iota(jnp.int32, (2 * BLOCK, inner), 0)
    row_hot = jnp.where(rows == row_ref[pl.ds(step, 1), :], 1.0, 0.0).astype(BF16)
    col_hot = jnp.where(cols == col_ref[pl.ds(step, 1), :], 1.0, 0.0).astype(BF16)
    counts = lax.dot_general(
        row_hot, col_hot, (((1,), (1,)), ((), ())), preferred_element_type=F32
    )
    return jnp.concatenate([counts[:OCT], counts[OCT:]], axis=1)


def count_kernel(row_ref, col_ref, out_ref, flag_ref):
    reader = pl.program_id(0)
    tops = []
    for d in range(DIRS):
        counts = counts_of(row_ref, col_ref, reader * DIRS + d)
        for s in range(RING):
            block = counts[:, s * BLOCK : (s + 1) * BLOCK]
            out_ref[s, 0, d * OCT : (d + 1) * OCT, :] = block.astype(BF16)
        tops.append(jnp.max(counts, axis=0, keepdims=True))
    large = jnp.max(functools.reduce(jnp.maximum, tops)) > 256.0
    flag_ref[reader] = large.astype(jnp.int32)


def count(row_codes, col_codes):
    codes = pl.BlockSpec(row_codes.shape, lambda k: (0, 0))
    return pl.pallas_call(
        count_kernel,
        grid=(RING,),
        in_specs=[codes, codes],
        out_specs=[pl.BlockSpec((RING, 1, DIRS * OCT, BLOCK), lambda k: (0, k, 0, 0)), SMEM],
        out_shape=[
            jax.ShapeDtypeStruct((RING, RING, DIRS * OCT, BLOCK), BF16),
            jax.ShapeDtypeStruct((RING,), jnp.int32),
        ],
        compiler_params=pltpu.CompilerParams(vmem_limit_bytes=12 << 20),
        cost_estimate=pl.CostEstimate(
            flops=100_000_000, bytes_accessed=1 << 20, transcendentals=0
        ),
        name="count",
    )(row_codes, col_codes)


def pick(ids_ref, first, refs, store):
    octants = lax.broadcasted_iota(jnp.int32, (OCT, RING * PER), 0)
    many = CORES * RING // len(refs)
    for i, ref in enumerate(refs):
        for j in range(many):
            owner = many * i + j
            table = jnp.concatenate(parts(ref[j * OCT : (j + 1) * OCT, :]), axis=1)
            hot = jnp.where(octants == ids_ref[first + owner : first + owner + 1, :], 1.0, 0.0)
            picked = lax.dot_general(
                hot.astype(BF16), table, (((0,), (0,)), ((), ())), preferred_element_type=F32
            ).astype(BF16)
            for k in range(RING):
                store(owner, k, picked[k * PER : (k + 1) * PER])


def gather_kernel(blocks, ids_ref, *refs):
    n = len(blocks)
    per = len(refs) // n - 1
    for i, s in enumerate(blocks):
        rows = refs[per * n + i]

        def store(owner, k, values, rows=rows):
            rows[k, owner * PER : (owner + 1) * PER, :] = values

        pick(ids_ref, s * 2 * RING, refs[per * i : per * (i + 1)], store)


def gather(blocks, ids, arrays):
    n = len(blocks)
    return pl.pallas_call(
        functools.partial(gather_kernel, blocks),
        in_specs=[VMEM] * (1 + len(arrays)),
        out_specs=[VMEM] * n,
        out_shape=[jax.ShapeDtypeStruct((RING, BLOCK, 2 * WIDTH), BF16)] * n,
        compiler_params=pltpu.CompilerParams(vmem_limit_bytes=6 << 20),
        cost_estimate=pl.CostEstimate(
            flops=n * 1_500_000_000, bytes_accessed=n << 20, transcendentals=0
        ),
        name="gather",
    )(ids, *arrays)


def product(counts, rows):
    both = jnp.dot(
        jnp.concatenate(counts, axis=1),
        jnp.concatenate(rows, axis=0),
        preferred_element_type=F32,
    )
    return both[:, :WIDTH] + both[:, WIDTH:]


def collect_kernel(blocks, first, count_ref, *refs):
    rows, out_ref = refs[: len(blocks)], refs[-1]

    @pl.loop(0, PAIR)
    def _(k):
        for m in range(0, DIRS, 2):
            here = slice(m * OCT, (m + 2) * OCT)
            out_ref[k, here, :] = product(
                [count_ref[s, first + k, here, :] for s in blocks],
                [ref[first + k] for ref in rows],
            )


def collect(blocks, first, counts, rows, kernels):
    n = len(blocks)
    return pl.pallas_call(
        functools.partial(collect_kernel, blocks, first),
        in_specs=[VMEM] * (1 + n + len(kernels)),
        out_specs=VMEM,
        out_shape=jax.ShapeDtypeStruct((PAIR, DIRS * OCT, WIDTH), F32),
        compiler_params=pltpu.CompilerParams(vmem_limit_bytes=8 << 20),
        cost_estimate=pl.CostEstimate(
            flops=n * 1_100_000_000, bytes_accessed=n << 20, transcendentals=0
        ),
        name="collect",
    )(counts, *rows, *kernels)


def finish_kernel(
    first, flag_ref, x_ref, rows0, rows1, rows2, rows3, count_ref, kh_ref, kl_ref,
    row_ref, col_ref, *refs,
):
    outs, xh, xl = refs[:-2], refs[-2], refs[-1]
    for i in range(len(outs)):
        k = first + i
        there = slice(i * OCT, (i + 1) * OCT)
        for m in range(0, DIRS, 2):
            here = slice(m * OCT, (m + 2) * OCT)
            old = x_ref[k % PAIR, here, :]
            total = old + product([count_ref[2, k, here, :]], [rows2[k]])
            high, low = parts(total)
            for j in range(2):
                xh[m + j, there, :] = high[j * OCT : (j + 1) * OCT]
                xl[m + j, there, :] = low[j * OCT : (j + 1) * OCT]

        @pl.when(flag_ref[k] != 0)
        def _():
            @pl.loop(0, DIRS)
            def _(d):
                exact = counts_of(row_ref, col_ref, k * DIRS + d)
                rest = (exact - exact.astype(BF16).astype(F32)).astype(BF16)
                rows = [ref[k] for ref in (rows0, rows1, rows2, rows3)]
                total = product([rest], rows)
                total += xh[d, there, :].astype(F32) + xl[d, there, :].astype(F32)
                high, low = parts(total)
                xh[d, there, :] = high
                xl[d, there, :] = low

    def dot(a, b):
        return jnp.dot(a, b, preferred_element_type=F32)

    total = None
    for d in range(DIRS):
        term = dot(xh[d], kh_ref[d]) + dot(xh[d], kl_ref[d]) + dot(xl[d], kh_ref[d])
        total = term if total is None else total + term
    for i, out in enumerate(outs):
        out[...] = total[i * OCT : (i + 1) * OCT]


def finish(first, n, flags, x, rows, counts, kernels, codes):
    return pl.pallas_call(
        functools.partial(finish_kernel, first),
        in_specs=[SMEM] + [VMEM] * 10,
        out_specs=[VMEM] * n,
        out_shape=[jax.ShapeDtypeStruct((OCT, WIDTH), F32)] * n,
        scratch_shapes=[pltpu.VMEM((DIRS, n * OCT, WIDTH), BF16)] * 2,
        compiler_params=pltpu.CompilerParams(vmem_limit_bytes=10 << 20),
        cost_estimate=pl.CostEstimate(
            flops=n * 3_000_000_000, bytes_accessed=2 << 20, transcendentals=0
        ),
        name="finish",
    )(flags, x, *rows, counts, *kernels, *codes)


def turn_kernel(k_ref, high_ref, low_ref):
    high_ref[0], low_ref[0] = parts(k_ref[0].T)


def turn(kernels):
    spec = pl.BlockSpec((1, WIDTH, WIDTH), lambda d: (d, 0, 0))
    return pl.pallas_call(
        turn_kernel,
        grid=(DIRS,),
        in_specs=[spec],
        out_specs=[spec] * 2,
        out_shape=[jax.ShapeDtypeStruct(kernels.shape, BF16)] * 2,
        compiler_params=pltpu.CompilerParams(vmem_limit_bytes=12 << 20),
        cost_estimate=pl.CostEstimate(
            flops=100_000_000, bytes_accessed=1 << 20, transcendentals=0
        ),
        name="turn",
    )(kernels)


def body(partials, partial_ids, read_lists, sources, targets, kernels):
    gx, gy = lax.axis_index("gx"), lax.axis_index("gy")
    device = gx * (RING * RING) + gy
    z, c, x, y = gx // CORES, gx % CORES, gy // RING, gy % RING
    owners = lax.axis_size(AXES)
    per_owner = partials.shape[0] // owners

    received = lax.all_to_all(partials, AXES, split_axis=0, concat_axis=0, tiled=True)

    number = jnp.arange(PLANE, dtype=jnp.int32)
    s, w, f = number // (RING * CORES), number // RING % CORES, number % RING
    core = (w + c) % CORES
    there_x = (x + jnp.where(core == 0, f, s)) % RING
    there_y = (y + jnp.where(core == 0, s, f)) % RING
    order = core * (RING * RING) + there_x * RING + there_y
    reads = [
        lax.dynamic_slice(
            read_lists,
            (((z + k) % RING * CORES + c) * (RING * RING) + gy, z * (PLANE * PER)),
            (1, PLANE * PER),
        )
        for k in ORDER
    ]
    reads = jnp.concatenate(reads, axis=0).reshape(RING, PLANE, PER)
    ids = jnp.take(reads.transpose(1, 0, 2).reshape(PLANE, RING * PER), order, axis=0)

    lists = jnp.concatenate([sources, targets], axis=0)
    ring_lists = {0: lists, **{k: along_z(lists, k) for k in range(1, RING)}}

    stacked = jnp.stack([ring_lists[k] for k in ORDER])
    slot, target = stacked[:, 0], stacked[:, 1]
    owner = slot // PER
    core = (owner // (RING * RING)) % CORES
    dx = (owner // RING - x) % RING
    dy = (owner - y) % RING
    s = jnp.where(core == 0, dy, dx)
    f = jnp.where(core == 0, dx, dy)
    column = ((s % 2 * CORES + (core + c) % CORES) * RING + f) * PER + slot % PER
    here = owner // PLANE == z
    row_codes = jnp.where(here, s // 2 * OCT + target, -1)
    per_dir = sources.shape[1] // DIRS
    codes = [code.reshape(RING * DIRS, per_dir) for code in (row_codes, column)]

    received, *kernels = lax.optimization_barrier((received, *turn(kernels)))
    octants = jnp.arange(OCT, dtype=jnp.int32)
    column_ids = lax.dynamic_slice_in_dim(partial_ids, device * per_owner, per_owner, 1).reshape(-1)
    selector = (octants[:, None] == column_ids[None, :]).astype(F32)
    density = jnp.dot(
        selector, received, precision=lax.Precision.HIGHEST, preferred_element_type=F32
    )

    line = [density] + [along_f(density, k) for k in range(1, RING)]
    line, codes, ids = lax.optimization_barrier((line, codes, ids))
    line = jnp.concatenate(line, axis=0)
    near1, near3 = along_s(line, 1), along_s(line, 3)
    counts, flags = count(*codes)
    near1, near3, counts, flags = lax.optimization_barrier((near1, near3, counts, flags))
    low, high = along_s(near1[: 2 * OCT], 1), along_s(near3[2 * OCT :], 3)
    (rows0,) = gather((0,), ids, [line, across(line)])
    rows1, rows3 = gather((1, 3), ids, [near1, across(near1), near3, across(near3)])
    rows = (rows0, rows1, rows3)
    x = [collect((0, 1, 3), 0, counts, rows, []), None]
    low, high, x[0], rows = lax.optimization_barrier((low, high, x[0], rows))
    far = [low, high, across(low), across(high)]
    x[1] = collect((0, 1, 3), PAIR, counts, rows, kernels)
    (rows2,) = gather((2,), ids, far)
    last = (rows[:2] + (rows2,) + rows[2:], counts, kernels, codes)
    (out2,) = finish(0, 1, flags, x[0], *last)
    ring2 = along_z(out2, -2)
    out1, out3 = finish(2, 2, flags, x[1], *last)
    ring1, ring3 = along_z(out1, -1), along_z(out3, -3)
    (out0,) = finish(1, 1, flags, x[0], *last)
    return out0 + ring2 + ring1 + ring3


def solution(mesh):
    return jax.shard_map(
        body,
        mesh=mesh,
        in_specs=(P(AXES, None), P(), P(), P(AXES, None), P(AXES, None), P()),
        out_specs=P(AXES, None),
        check_vma=False,
    )
```

```python
import functools

import jax
import jax.numpy as jnp
from jax import lax
from jax.experimental import pallas as pl
from jax.experimental.pallas import tpu as pltpu
from jax.sharding import PartitionSpec as P

AXES = ("gx", "gy")
RING = 4
CORES = 2
OCT = 128
PER = 32
DIRS = 8
WIDTH = 512
PLANE = RING * RING * CORES
BLOCK = CORES * RING * PER
BF16 = jnp.bfloat16
F32 = jnp.float32
SMEM = pl.BlockSpec(memory_space=pltpu.SMEM)
VMEM = pl.BlockSpec(memory_space=pltpu.VMEM)
PAIR = 2
ORDER = (2, 0, 1, 3)


def device_of(x, y, z, c):
    return ((z % RING) * CORES + c % CORES) * RING * RING + (x % RING) * RING + y % RING


def fetch(value, shift):
    pairs = []
    for z in range(RING):
        for c in range(CORES):
            for x in range(RING):
                for y in range(RING):
                    dx, dy, dz, dc = shift(c)
                    pairs.append((device_of(x + dx, y + dy, z + dz, c + dc), device_of(x, y, z, c)))
    return lax.ppermute(value, AXES, pairs)


def along_f(value, k):
    return fetch(value, lambda core: (k, 0, 0, 0) if core == 0 else (0, k, 0, 0))


def along_s(value, k):
    return fetch(value, lambda core: (0, k, 0, 0) if core == 0 else (k, 0, 0, 0))


def along_z(value, k):
    return fetch(value, lambda core: (0, 0, k, 0))


def across(value):
    return fetch(value, lambda core: (0, 0, 0, 1))


def parts(value):
    high = value.astype(BF16)
    return high, (value - high.astype(F32)).astype(BF16)


def counts_of(row_ref, col_ref, step):
    inner = row_ref.shape[1]
    rows = lax.broadcasted_iota(jnp.int32, (RING // 2 * OCT, inner), 0)
    cols = lax.broadcasted_iota(jnp.int32, (2 * BLOCK, inner), 0)
    row_hot = jnp.where(rows == row_ref[pl.ds(step, 1), :], 1.0, 0.0).astype(BF16)
    col_hot = jnp.where(cols == col_ref[pl.ds(step, 1), :], 1.0, 0.0).astype(BF16)
    counts = lax.dot_general(
        row_hot, col_hot, (((1,), (1,)), ((), ())), preferred_element_type=F32
    )
    return jnp.concatenate([counts[:OCT], counts[OCT:]], axis=1)


def count_kernel(row_ref, col_ref, out_ref, flag_ref):
    reader = pl.program_id(0)
    tops = []
    for d in range(DIRS):
        counts = counts_of(row_ref, col_ref, reader * DIRS + d)
        for s in range(RING):
            block = counts[:, s * BLOCK : (s + 1) * BLOCK]
            out_ref[s, 0, d * OCT : (d + 1) * OCT, :] = block.astype(BF16)
        tops.append(jnp.max(counts, axis=0, keepdims=True))
    large = jnp.max(functools.reduce(jnp.maximum, tops)) > 256.0
    flag_ref[reader] = large.astype(jnp.int32)


def count(row_codes, col_codes):
    codes = pl.BlockSpec(row_codes.shape, lambda k: (0, 0))
    return pl.pallas_call(
        count_kernel,
        grid=(RING,),
        in_specs=[codes, codes],
        out_specs=[pl.BlockSpec((RING, 1, DIRS * OCT, BLOCK), lambda k: (0, k, 0, 0)), SMEM],
        out_shape=[
            jax.ShapeDtypeStruct((RING, RING, DIRS * OCT, BLOCK), BF16),
            jax.ShapeDtypeStruct((RING,), jnp.int32),
        ],
        compiler_params=pltpu.CompilerParams(vmem_limit_bytes=12 << 20),
        cost_estimate=pl.CostEstimate(
            flops=100_000_000, bytes_accessed=1 << 20, transcendentals=0
        ),
        name="count",
    )(row_codes, col_codes)


def pick(ids_ref, first, refs, store):
    octants = lax.broadcasted_iota(jnp.int32, (OCT, RING * PER), 0)
    many = CORES * RING // len(refs)
    for i, ref in enumerate(refs):
        for j in range(many):
            owner = many * i + j
            table = jnp.concatenate(parts(ref[j * OCT : (j + 1) * OCT, :]), axis=1)
            hot = jnp.where(octants == ids_ref[first + owner : first + owner + 1, :], 1.0, 0.0)
            picked = lax.dot_general(
                hot.astype(BF16), table, (((0,), (0,)), ((), ())), preferred_element_type=F32
            ).astype(BF16)
            for k in range(RING):
                store(owner, k, picked[k * PER : (k + 1) * PER])


def gather_kernel(blocks, ids_ref, *refs):
    n = len(blocks)
    per = len(refs) // n - 1
    for i, s in enumerate(blocks):
        rows = refs[per * n + i]

        def store(owner, k, values, rows=rows):
            rows[k, owner * PER : (owner + 1) * PER, :] = values

        pick(ids_ref, s * 2 * RING, refs[per * i : per * (i + 1)], store)


def gather(blocks, ids, arrays):
    n = len(blocks)
    return pl.pallas_call(
        functools.partial(gather_kernel, blocks),
        in_specs=[VMEM] * (1 + len(arrays)),
        out_specs=[VMEM] * n,
        out_shape=[jax.ShapeDtypeStruct((RING, BLOCK, 2 * WIDTH), BF16)] * n,
        compiler_params=pltpu.CompilerParams(vmem_limit_bytes=6 << 20),
        cost_estimate=pl.CostEstimate(
            flops=n * 1_500_000_000, bytes_accessed=n << 20, transcendentals=0
        ),
        name="gather",
    )(ids, *arrays)


def product(counts, rows):
    both = jnp.dot(
        jnp.concatenate(counts, axis=1),
        jnp.concatenate(rows, axis=0),
        preferred_element_type=F32,
    )
    return both[:, :WIDTH] + both[:, WIDTH:]


def collect_kernel(blocks, first, count_ref, *refs):
    rows, out_ref = refs[: len(blocks)], refs[-1]

    @pl.loop(0, PAIR)
    def _(k):
        for m in range(0, DIRS, 2):
            here = slice(m * OCT, (m + 2) * OCT)
            out_ref[k, here, :] = product(
                [count_ref[s, first + k, here, :] for s in blocks],
                [ref[first + k] for ref in rows],
            )


def collect(blocks, first, counts, rows, kernels):
    n = len(blocks)
    return pl.pallas_call(
        functools.partial(collect_kernel, blocks, first),
        in_specs=[VMEM] * (1 + n + len(kernels)),
        out_specs=VMEM,
        out_shape=jax.ShapeDtypeStruct((PAIR, DIRS * OCT, WIDTH), F32),
        compiler_params=pltpu.CompilerParams(vmem_limit_bytes=8 << 20),
        cost_estimate=pl.CostEstimate(
            flops=n * 1_100_000_000, bytes_accessed=n << 20, transcendentals=0
        ),
        name="collect",
    )(counts, *rows, *kernels)


def finish_kernel(
    first, flag_ref, x_ref, rows0, rows1, rows2, rows3, count_ref, kh_ref, kl_ref,
    row_ref, col_ref, *refs,
):
    outs, xh, xl = refs[:-2], refs[-2], refs[-1]
    for i in range(len(outs)):
        k = first + i
        there = slice(i * OCT, (i + 1) * OCT)
        for m in range(0, DIRS, 2):
            here = slice(m * OCT, (m + 2) * OCT)
            old = x_ref[k % PAIR, here, :]
            total = old + product([count_ref[2, k, here, :]], [rows2[k]])
            high, low = parts(total)
            for j in range(2):
                xh[m + j, there, :] = high[j * OCT : (j + 1) * OCT]
                xl[m + j, there, :] = low[j * OCT : (j + 1) * OCT]

        @pl.when(flag_ref[k] != 0)
        def _():
            @pl.loop(0, DIRS)
            def _(d):
                exact = counts_of(row_ref, col_ref, k * DIRS + d)
                rest = (exact - exact.astype(BF16).astype(F32)).astype(BF16)
                rows = [ref[k] for ref in (rows0, rows1, rows2, rows3)]
                total = product([rest], rows)
                total += xh[d, there, :].astype(F32) + xl[d, there, :].astype(F32)
                high, low = parts(total)
                xh[d, there, :] = high
                xl[d, there, :] = low

    def dot(a, b):
        return jnp.dot(a, b, preferred_element_type=F32)

    total = None
    for d in range(DIRS):
        term = dot(xh[d], kh_ref[d]) + dot(xh[d], kl_ref[d]) + dot(xl[d], kh_ref[d])
        total = term if total is None else total + term
    for i, out in enumerate(outs):
        out[...] = total[i * OCT : (i + 1) * OCT]


def finish(first, n, flags, x, rows, counts, kernels, codes):
    return pl.pallas_call(
        functools.partial(finish_kernel, first),
        in_specs=[SMEM] + [VMEM] * 10,
        out_specs=[VMEM] * n,
        out_shape=[jax.ShapeDtypeStruct((OCT, WIDTH), F32)] * n,
        scratch_shapes=[pltpu.VMEM((DIRS, n * OCT, WIDTH), BF16)] * 2,
        compiler_params=pltpu.CompilerParams(vmem_limit_bytes=10 << 20),
        cost_estimate=pl.CostEstimate(
            flops=n * 3_000_000_000, bytes_accessed=2 << 20, transcendentals=0
        ),
        name="finish",
    )(flags, x, *rows, counts, *kernels, *codes)


def turn_kernel(k_ref, high_ref, low_ref):
    high_ref[0], low_ref[0] = parts(k_ref[0].T)


def turn(kernels):
    spec = pl.BlockSpec((1, WIDTH, WIDTH), lambda d: (d, 0, 0))
    return pl.pallas_call(
        turn_kernel,
        grid=(DIRS,),
        in_specs=[spec],
        out_specs=[spec] * 2,
        out_shape=[jax.ShapeDtypeStruct(kernels.shape, BF16)] * 2,
        compiler_params=pltpu.CompilerParams(vmem_limit_bytes=12 << 20),
        cost_estimate=pl.CostEstimate(
            flops=100_000_000, bytes_accessed=1 << 20, transcendentals=0
        ),
        name="turn",
    )(kernels)


def body(partials, partial_ids, read_lists, sources, targets, kernels):
    gx, gy = lax.axis_index("gx"), lax.axis_index("gy")
    device = gx * (RING * RING) + gy
    z, c, x, y = gx // CORES, gx % CORES, gy // RING, gy % RING
    owners = lax.axis_size(AXES)
    per_owner = partials.shape[0] // owners

    received = lax.all_to_all(partials, AXES, split_axis=0, concat_axis=0, tiled=True)

    number = jnp.arange(PLANE, dtype=jnp.int32)
    s, w, f = number // (RING * CORES), number // RING % CORES, number % RING
    core = (w + c) % CORES
    there_x = (x + jnp.where(core == 0, f, s)) % RING
    there_y = (y + jnp.where(core == 0, s, f)) % RING
    order = core * (RING * RING) + there_x * RING + there_y
    reads = [
        lax.dynamic_slice(
            read_lists,
            (((z + k) % RING * CORES + c) * (RING * RING) + gy, z * (PLANE * PER)),
            (1, PLANE * PER),
        )
        for k in ORDER
    ]
    reads = jnp.concatenate(reads, axis=0).reshape(RING, PLANE, PER)
    ids = jnp.take(reads.transpose(1, 0, 2).reshape(PLANE, RING * PER), order, axis=0)

    lists = jnp.concatenate([sources, targets], axis=0)
    ring_lists = {0: lists, **{k: along_z(lists, k) for k in range(1, RING)}}

    stacked = jnp.stack([ring_lists[k] for k in ORDER])
    slot, target = stacked[:, 0], stacked[:, 1]
    owner = slot // PER
    core = (owner // (RING * RING)) % CORES
    dx = (owner // RING - x) % RING
    dy = (owner - y) % RING
    s = jnp.where(core == 0, dy, dx)
    f = jnp.where(core == 0, dx, dy)
    column = ((s % 2 * CORES + (core + c) % CORES) * RING + f) * PER + slot % PER
    here = owner // PLANE == z
    row_codes = jnp.where(here, s // 2 * OCT + target, -1)
    per_dir = sources.shape[1] // DIRS
    codes = [code.reshape(RING * DIRS, per_dir) for code in (row_codes, column)]

    received, *kernels = lax.optimization_barrier((received, *turn(kernels)))
    octants = jnp.arange(OCT, dtype=jnp.int32)
    column_ids = lax.dynamic_slice_in_dim(partial_ids, device * per_owner, per_owner, 1).reshape(-1)
    selector = (octants[:, None] == column_ids[None, :]).astype(F32)
    density = jnp.dot(
        selector, received, precision=lax.Precision.HIGHEST, preferred_element_type=F32
    )

    line = [density] + [along_f(density, k) for k in range(1, RING)]
    line, codes, ids = lax.optimization_barrier((line, codes, ids))
    line = jnp.concatenate(line, axis=0)
    near1, near3 = along_s(line, 1), along_s(line, 3)
    counts, flags = count(*codes)
    near1, near3, counts, flags = lax.optimization_barrier((near1, near3, counts, flags))
    low, high = along_s(near1[: 2 * OCT], 1), along_s(near3[2 * OCT :], 3)
    near = [line, across(line), near1, across(near1), near3, across(near3)]
    rows0, rows1, rows3 = gather((0, 1, 3), ids, near)
    rows = (rows0, rows1, rows3)
    x = [collect((0, 1, 3), 0, counts, rows, []), None]
    low, high, x[0], rows = lax.optimization_barrier((low, high, x[0], rows))
    far = [low, high, across(low), across(high)]
    x[1] = collect((0, 1, 3), PAIR, counts, rows, kernels)
    (rows2,) = gather((2,), ids, far)
    last = (rows[:2] + (rows2,) + rows[2:], counts, kernels, codes)
    (out2,) = finish(0, 1, flags, x[0], *last)
    ring2 = along_z(out2, -2)
    out1, out3 = finish(2, 2, flags, x[1], *last)
    ring1, ring3 = along_z(out1, -1), along_z(out3, -3)
    (out0,) = finish(1, 1, flags, x[0], *last)
    return out0 + ring2 + ring1 + ring3


def solution(mesh):
    return jax.shard_map(
        body,
        mesh=mesh,
        in_specs=(P(AXES, None), P(), P(), P(AXES, None), P(AXES, None), P()),
        out_specs=P(AXES, None),
        check_vma=False,
    )
```
